512 devices in a mesh: row: 16 (over y, core), col: 32 (over x, z).
Axes of the slice: x: 4, y: 8, z: 8, core: 2. Of those that a mesh axis runs over, the one named last changes fastest.
Arguments:
- rhs: bfloat16 [4, 16, 32, 64, 256], P(None, 'row', 'col'), may hold values from -6 to 6
- dinv: float32 [4, 16, 32, 64, 64], P(None, 'row', 'col'), may hold values from -1.5 to 1.5, as said below
- lower: bfloat16 [6, 16, 32, 32, 64, 128], P(None, 'row', 'col'), may hold values from -0.0625 to 0.0625
- sources: int32 [6, 16, 32, 32, 2], P(None, 'row', 'col'), may hold values from -1 to 15, as said below
Outputs:
- solution: float32 [4, 16, 32, 64, 256], P(None, 'row', 'col')
The draws below stay inside these ranges and needn't reach their ends.
Inputs may be any that keep to these rules, and one draw needn't show every extreme that they name: `dinv`: lower triangular. `sources`: for each level pair, holder and target, the live entries are distinct; in every level pair every device has a target with all 2 entries live.
All inputs are finite; a program needn't handle non-finite values.
Results may differ from the reference program's by a relative error of at most 0.002.
Values may be sent and summed in bfloat16 or wider, within the bound.
No kernel may reach another device: no remote copies, remote signals or barrier semaphores. Data moves between devices by JAX's collectives and lax.ppermute only.
A program may use at most 64 MiB of HBM per device.

```python
import jax
import jax.numpy as jnp
from jax import lax

BS = 64
RHS = 256
LEVELS = 4
PER = 2
NR = 16
NC = 32
PAIRS = 6


def draw_dinv(key, part):
    key = jax.random.fold_in(key, 11)
    first, second = jax.random.split(key)
    shape = (LEVELS, NR, NC, BS, BS)
    below = jnp.arange(BS)[:, None] > jnp.arange(BS)[None, :]
    diagonal_mask = jnp.arange(BS)[:, None] == jnp.arange(BS)[None, :]
    spread = jnp.clip(jax.random.normal(first, shape, jnp.float32), -4.0, 4.0) * (0.5 / BS ** 0.5)
    diagonal = jax.random.uniform(second, shape[:-1], jnp.float32, 0.6, 1.4)
    return jnp.where(below, spread, 0.0) + jnp.where(diagonal_mask, diagonal[..., None], 0.0)


def draw_sources(key, part):
    key = jax.random.fold_in(key, 23)
    first, second, third = jax.random.split(key, 3)
    scores = jax.random.randint(first, (PAIRS, NR, NC, NC, NR), 0, 1 << 20) * NR + jnp.arange(NR, dtype=jnp.int32)
    ordering = jnp.argsort(scores, axis=-1)[..., :PER].astype(jnp.int32)
    counts = jax.random.randint(second, (PAIRS, NR, NC, NC), 0, PER + 1)
    filled = jax.random.randint(third, (PAIRS, NR, NC), 0, NC)
    counts = jnp.where(jnp.arange(NC) == filled[..., None], PER, counts)
    live = jnp.arange(PER) < counts[..., None]
    return jnp.where(live, ordering, -1).astype(jnp.int32)


def steps_of(own_key, dims, shards, least, top_value):
    def one(axis_at, blocks):
        heights = jax.random.uniform(jax.random.fold_in(jax.random.fold_in(own_key, 6), axis_at), (blocks,), jnp.float32, least / len(shards), top_value / len(shards))
        return jnp.repeat(jnp.exp(heights), dims[axis_at] // blocks).reshape((-1,) + (1,) * (len(dims) - axis_at - 1))

    level = one(*shards[0])
    for cut in shards[1:]:
        level = level * one(*cut)
    return level


def gaussian(rng, shape, width, most, pieces=(), kind=jnp.bfloat16):
    result = width * jax.random.normal(rng, shape, jnp.float32)
    if pieces:
        result = result * steps_of(rng, shape, pieces, -0.22, 0.18)
    return jnp.clip(result, -most, most).astype(kind)


def setup_inputs(seed: int = 0) -> dict:
    key_of = jax.random.split(jax.random.key(seed), 5)
    rhs = gaussian(key_of[0], (LEVELS, NR, NC, BS, RHS), 1.0, 6.0, ((1, 16), (2, 32)))
    dinv = draw_dinv(jax.random.fold_in(key_of[4], 71), 0)
    lower = gaussian(key_of[2], (PAIRS, NR, NC, NC, BS, PER * BS), (4 * BS * NC) ** -0.5, 0.0625, ((1, 16), (2, 32)))
    sources = draw_sources(jax.random.fold_in(key_of[4], 71), 0)
    return {"rhs": rhs, "dinv": dinv, "lower": lower, "sources": sources}


def level_update(lower_pair, source_pair, solved):
    column_ids = jnp.arange(NC, dtype=jnp.int32)[:, None, None]

    def row_update(items):
        blocks, indices = items
        clipped = jnp.maximum(indices, 0).astype(jnp.int32)
        picked = solved[clipped, column_ids]
        picked = jnp.where((indices >= 0)[..., None, None], picked.astype(jnp.float32), jnp.float32(0.0))
        picked = picked.reshape(NC, NC, PER * BS, RHS)
        return jnp.einsum("cqik,cqkn->qin", blocks.astype(jnp.float32), picked)

    return lax.map(row_update, (lower_pair, source_pair))


def reference(rhs, dinv, lower, sources):
    accumulated = [jnp.zeros((NR, NC, BS, RHS), jnp.float32) for section in range(LEVELS)]
    results = []
    pair_index = 0
    for section in range(LEVELS):
        residual = rhs[section].astype(jnp.float32) - accumulated[section]
        solution = jnp.einsum("rcij,rcjn->rcin", dinv[section], residual, precision=lax.Precision.HIGHEST)
        results.append(solution)
        solved = solution.astype(jnp.bfloat16)
        for target in range(section + 1, LEVELS):
            accumulated[target] = accumulated[target] + level_update(lower[pair_index], sources[pair_index], solved)
            pair_index += 1
    return jnp.stack(results)
```

```python
import jax
import jax.numpy as jnp
from jax import lax
from jax.sharding import PartitionSpec as P


def level_terms(blocks, indices, gathered):
    clipped = jnp.maximum(indices, 0)
    picked = jnp.take(gathered, clipped, axis=0)
    picked = jnp.where((indices >= 0)[:, :, None, None], picked, jnp.zeros((), gathered.dtype))
    peer_count, per_count, block_rows, rhs_width = picked.shape
    picked = picked.reshape(peer_count, per_count * block_rows, rhs_width)
    return jnp.einsum("qik,qkn->qin", blocks, picked, preferred_element_type=jnp.float32)


def on_device(rhs, dinv, lower, sources):
    levels = rhs.shape[0]
    pair_of = {}
    for section in range(levels):
        for target in range(section + 1, levels):
            pair_of[section, target] = len(pair_of)
    gathered = []
    results = []
    for section in range(levels):
        residual = rhs[section, 0, 0].astype(jnp.float32)
        if section:
            partial = None
            for earlier in range(section):
                pair = pair_of[earlier, section]
                term = level_terms(lower[pair, 0, 0], sources[pair, 0, 0], gathered[earlier])
                partial = term if partial is None else partial + term
            arrived = lax.all_to_all(
                partial.astype(jnp.bfloat16), "col", split_axis=0, concat_axis=0, tiled=True
            )
            residual = residual - jnp.sum(arrived.astype(jnp.float32), axis=0)
        solution = jnp.dot(
            dinv[section, 0, 0],
            residual,
            precision=lax.Precision.HIGHEST,
            preferred_element_type=jnp.float32,
        )
        results.append(solution)
        if section + 1 < levels:
            solved = solution.astype(jnp.bfloat16)
            gathered.append(lax.all_gather(solved[None], "row", axis=0, tiled=True))
    return jnp.stack(results)[:, None, None]


def solution(mesh):
    in_specs = (
        P(None, "row", "col", None, None),
        P(None, "row", "col", None, None),
        P(None, "row", "col", None, None, None),
        P(None, "row", "col", None, None),
    )
    out_specs = P(None, "row", "col", None, None)
    return jax.shard_map(
        on_device, mesh=mesh, in_specs=in_specs, out_specs=out_specs, check_vma=False
    )
```

```python
import functools

import jax
import jax.numpy as jnp
from jax import lax
from jax.experimental import pallas as pl
from jax.experimental.pallas import tpu as pltpu
from jax.sharding import PartitionSpec as P

LANES = 128
PAD = 8
VMEM = pl.BlockSpec(memory_space=pltpu.VMEM)


def terms_kernel(pairs, sources_ref, lower_ref, *refs):
    gathered, out_ref = refs[:-1], refs[-1]
    _, targets, block_rows, depth = lower_ref.shape
    per = depth // block_rows
    halves = gathered[0].shape[2] // LANES
    tail = halves * block_rows

    def one(target, carry):
        factors, picked = [], []
        for block, pair in zip(gathered, pairs):
            factors.append(lower_ref[pair, target])
            for entry in range(per):
                source = sources_ref[(pair * targets + target) * per + entry]
                rows = block[jnp.maximum(source, 0)]
                picked.append(jnp.where(source >= 0, rows, jnp.zeros_like(rows)))
        term = jnp.dot(
            jnp.concatenate(factors, axis=1),
            jnp.concatenate(picked, axis=0),
            preferred_element_type=jnp.float32,
        )
        powers = []
        for half in range(halves):
            part = term[:, half * LANES : (half + 1) * LANES]
            largest = jnp.max(jnp.abs(part), axis=0, keepdims=True)
            power = jnp.ceil(jnp.log2(jnp.maximum(largest * 1.001, 1e-30)))
            coded = jnp.floor(part * jnp.exp2(15.0 - power) + 0.5)
            out_ref[target, half * block_rows : (half + 1) * block_rows, :] = coded.astype(
                jnp.int32
            ).astype(jnp.int16)
            powers.append(jnp.broadcast_to(power, (PAD // halves, LANES)))
        powers = jnp.concatenate(powers, axis=0)
        out_ref[target, tail : tail + PAD, :] = powers.astype(jnp.int32).astype(jnp.int16)
        return carry

    lax.fori_loop(0, targets, one, 0, unroll=8)


def local_terms(pairs, sources, lower, gathered):
    _, targets, block_rows, _ = lower.shape
    halves = gathered[0].shape[2] // LANES
    rows = halves * block_rows + PAD
    return pl.pallas_call(
        functools.partial(terms_kernel, pairs),
        out_shape=jax.ShapeDtypeStruct((targets, rows, LANES), jnp.int16),
        in_specs=[pl.BlockSpec(memory_space=pltpu.SMEM)] + [VMEM] * (1 + len(gathered)),
        out_specs=VMEM,
        name="local_terms",
    )(sources, lower, *gathered)


def solve_level(section, rhs_ref, dinv_ref, arrived_ref):
    peers, _, _ = arrived_ref.shape
    block_rows, width = rhs_ref.shape[1:]
    halves = width // LANES
    tail = halves * block_rows

    def add(peer, sums):
        scales = arrived_ref[peer, tail : tail + PAD, :].astype(jnp.int32).astype(jnp.float32)
        scales = jnp.exp2(scales - 15.0)
        added = []
        for half in range(halves):
            coded = arrived_ref[peer, half * block_rows : (half + 1) * block_rows, :]
            first = half * (PAD // halves)
            scale = scales[first : first + 1, :]
            added.append(sums[half] + coded.astype(jnp.int32).astype(jnp.float32) * scale)
        return tuple(added)

    zero = jnp.zeros((block_rows, LANES), jnp.float32)
    sums = lax.fori_loop(0, peers, add, (zero,) * halves, unroll=4)
    residual = rhs_ref[section].astype(jnp.float32) - jnp.concatenate(sums, axis=1)
    return jnp.dot(
        dinv_ref[section],
        residual,
        precision=lax.Precision.HIGHEST,
        preferred_element_type=jnp.float32,
    )


def middle_kernel(section, rhs_ref, dinv_ref, arrived_ref, solution_ref, solved_ref):
    result = solve_level(section, rhs_ref, dinv_ref, arrived_ref)
    solution_ref[...] = result
    solved_ref[...] = result.astype(jnp.bfloat16)


def last_kernel(rhs_ref, dinv_ref, arrived_ref, *refs):
    earlier, out_ref, result_ref, sems = refs[:-3], refs[-3], refs[-2], refs[-1]
    section = len(earlier)
    copies = [
        pltpu.make_async_copy(ref, out_ref.at[level], sems.at[level])
        for level, ref in enumerate(earlier)
    ]
    for copy in copies:
        copy.start()
    result_ref[...] = solve_level(section, rhs_ref, dinv_ref, arrived_ref)
    copies.append(pltpu.make_async_copy(result_ref, out_ref.at[section], sems.at[section]))
    copies[-1].start()
    for copy in copies:
        copy.wait()


def solve_middle(section, rhs, dinv, arrived):
    _, block_rows, width = rhs.shape
    return pl.pallas_call(
        functools.partial(middle_kernel, section),
        out_shape=(
            jax.ShapeDtypeStruct((block_rows, width), jnp.float32),
            jax.ShapeDtypeStruct((block_rows, width), jnp.bfloat16),
        ),
        in_specs=[VMEM] * 3,
        out_specs=(VMEM, VMEM),
        name="solve_middle",
    )(rhs, dinv, arrived)


def solve_last(rhs, dinv, arrived, earlier):
    levels, block_rows, width = rhs.shape
    return pl.pallas_call(
        last_kernel,
        out_shape=jax.ShapeDtypeStruct((levels, block_rows, width), jnp.float32),
        in_specs=[VMEM] * (3 + len(earlier)),
        out_specs=pl.BlockSpec(memory_space=pl.ANY),
        scratch_shapes=[
            pltpu.VMEM((block_rows, width), jnp.float32),
            pltpu.SemaphoreType.DMA((levels,)),
        ],
        name="solve_last",
    )(rhs, dinv, arrived, *earlier)


def on_device(rhs, dinv, lower, sources):
    levels = rhs.shape[0]
    pair_of = {}
    for section in range(levels):
        for target in range(section + 1, levels):
            pair_of[section, target] = len(pair_of)
    rhs, dinv, lower = rhs[:, 0, 0], dinv[:, 0, 0], lower[:, 0, 0]
    sources = sources.reshape(-1)
    solution = jnp.dot(
        dinv[0],
        rhs[0].astype(jnp.float32),
        precision=lax.Precision.HIGHEST,
        preferred_element_type=jnp.float32,
    )
    solved = solution.astype(jnp.bfloat16)
    solutions, gathered = [solution], []
    for section in range(1, levels):
        gathered.append(lax.all_gather(solved, "row", axis=0, tiled=False))
        pairs = tuple(pair_of[earlier, section] for earlier in range(section))
        coded = local_terms(pairs, sources, lower, gathered)
        arrived = lax.all_to_all(coded, "col", split_axis=0, concat_axis=0, tiled=True)
        if section + 1 < levels:
            solution, solved = solve_middle(section, rhs, dinv, arrived)
            solutions.append(solution)
        else:
            stacked = solve_last(rhs, dinv, arrived, solutions)
    return stacked[:, None, None]


def solution(mesh):
    in_specs = (
        P(None, "row", "col", None, None),
        P(None, "row", "col", None, None),
        P(None, "row", "col", None, None, None),
        P(None, "row", "col", None, None),
    )
    out_specs = P(None, "row", "col", None, None)
    return jax.shard_map(
        on_device, mesh=mesh, in_specs=in_specs, out_specs=out_specs, check_vma=False
    )
```

```python
import functools

import jax
import jax.numpy as jnp
from jax import lax
from jax.experimental import pallas as pl
from jax.experimental.pallas import tpu as pltpu
from jax.sharding import PartitionSpec as P

LANES = 128
PAD = 8
KERNEL_VMEM = 8 << 20
CHUNKS = 4
VMEM = pl.BlockSpec(memory_space=pltpu.VMEM)


def in_vmem(array):
    return pltpu.with_memory_space_constraint(array, pltpu.VMEM)


def in_hbm(array):
    return pltpu.with_memory_space_constraint(array, pltpu.HBM)


def terms_kernel(pairs, sources_ref, lower_ref, *refs):
    gathered, (out_ref, factors_ref, sems) = refs[:-3], refs[-3:]
    _, targets, block_rows, depth = lower_ref.shape
    chunk = targets // CHUNKS
    copies = [
        [
            pltpu.make_async_copy(
                lower_ref.at[pair, pl.ds(step * chunk, chunk)],
                factors_ref.at[place, pl.ds(step * chunk, chunk)],
                sems.at[step, place],
            )
            for place, pair in enumerate(pairs)
        ]
        for step in range(CHUNKS)
    ]
    for step in range(CHUNKS):
        for copy in copies[step]:
            copy.start()
    per = depth // block_rows
    halves = gathered[0].shape[2] // LANES
    tail = halves * block_rows

    def one(target, carry):
        factors, picked = [], []
        for place, (block, pair) in enumerate(zip(gathered, pairs)):
            factors.append(factors_ref[place, target])
            for entry in range(per):
                source = sources_ref[pair, entry, target]
                rows = block[jnp.maximum(source, 0)]
                picked.append(jnp.where(source >= 0, rows, jnp.zeros_like(rows)))
        term = jnp.dot(
            jnp.concatenate(factors, axis=1),
            jnp.concatenate(picked, axis=0),
            preferred_element_type=jnp.float32,
        )
        powers = []
        for half in range(halves):
            part = term[:, half * LANES : (half + 1) * LANES]
            largest = jnp.max(jnp.abs(part), axis=0, keepdims=True)
            power = jnp.ceil(jnp.log2(jnp.maximum(largest * 1.001, 1e-30)))
            coded = jnp.floor(part * jnp.exp2(15.0 - power) + 0.5)
            out_ref[target, half * block_rows : (half + 1) * block_rows, :] = coded.astype(
                jnp.int32
            ).astype(jnp.int16)
            powers.append(jnp.broadcast_to(power, (PAD // halves, LANES)))
        powers = jnp.concatenate(powers, axis=0)
        out_ref[target, tail : tail + PAD, :] = powers.astype(jnp.int32).astype(jnp.int16)
        return carry

    for step in range(CHUNKS):
        for copy in copies[step]:
            copy.wait()
        lax.fori_loop(step * chunk, (step + 1) * chunk, one, 0, unroll=True)


def local_terms(pairs, sources, lower, gathered):
    _, targets, block_rows, depth = lower.shape
    halves = gathered[0].shape[2] // LANES
    rows = halves * block_rows + PAD
    return pl.pallas_call(
        functools.partial(terms_kernel, pairs),
        out_shape=pltpu.VMEM((targets, rows, LANES), jnp.int16),
        in_specs=[pl.BlockSpec(memory_space=pltpu.SMEM), pl.BlockSpec(memory_space=pl.ANY)]
        + [VMEM] * len(gathered),
        out_specs=VMEM,
        scratch_shapes=[
            pltpu.VMEM((len(pairs), targets, block_rows, depth), lower.dtype),
            pltpu.SemaphoreType.DMA((CHUNKS, len(pairs))),
        ],
        compiler_params=pltpu.CompilerParams(vmem_limit_bytes=KERNEL_VMEM),
        name="local_terms",
    )(in_hbm(sources), in_hbm(lower), *map(in_vmem, gathered))


def solve_level(section, rhs_ref, dinv_ref, arrived_ref):
    peers, _, _ = arrived_ref.shape
    block_rows, width = rhs_ref.shape[1:]
    halves = width // LANES
    tail = halves * block_rows

    def add(peer, sums):
        scales = arrived_ref[peer, tail : tail + PAD, :].astype(jnp.int32).astype(jnp.float32)
        scales = jnp.exp2(scales - 15.0)
        added = []
        for half in range(halves):
            coded = arrived_ref[peer, half * block_rows : (half + 1) * block_rows, :]
            first = half * (PAD // halves)
            scale = scales[first : first + 1, :]
            added.append(sums[half] + coded.astype(jnp.int32).astype(jnp.float32) * scale)
        return tuple(added)

    zero = jnp.zeros((block_rows, LANES), jnp.float32)
    sums = lax.fori_loop(0, peers, add, (zero,) * halves, unroll=4)
    residual = rhs_ref[section].astype(jnp.float32) - jnp.concatenate(sums, axis=1)
    return jnp.dot(
        dinv_ref[section],
        residual,
        precision=lax.Precision.HIGHEST,
        preferred_element_type=jnp.float32,
    )


def middle_kernel(section, rhs_ref, dinv_ref, arrived_ref, solution_ref, solved_ref):
    result = solve_level(section, rhs_ref, dinv_ref, arrived_ref)
    solution_ref[...] = result
    solved_ref[...] = result.astype(jnp.bfloat16)


def last_kernel(rhs_ref, dinv_ref, arrived_ref, *refs):
    earlier, out_ref, result_ref, sems = refs[:-3], refs[-3], refs[-2], refs[-1]
    section = len(earlier)
    copies = [
        pltpu.make_async_copy(ref, out_ref.at[level], sems.at[level])
        for level, ref in enumerate(earlier)
    ]
    for copy in copies:
        copy.start()
    result_ref[...] = solve_level(section, rhs_ref, dinv_ref, arrived_ref)
    copies.append(pltpu.make_async_copy(result_ref, out_ref.at[section], sems.at[section]))
    copies[-1].start()
    for copy in copies:
        copy.wait()


def solve_middle(section, rhs, dinv, arrived):
    _, block_rows, width = rhs.shape
    return pl.pallas_call(
        functools.partial(middle_kernel, section),
        out_shape=(
            pltpu.VMEM((block_rows, width), jnp.float32),
            pltpu.VMEM((block_rows, width), jnp.bfloat16),
        ),
        in_specs=[VMEM] * 3,
        out_specs=(VMEM, VMEM),
        compiler_params=pltpu.CompilerParams(vmem_limit_bytes=KERNEL_VMEM),
        name="solve_middle",
    )(*map(in_vmem, (rhs, dinv, arrived)))


def solve_last(rhs, dinv, arrived, earlier):
    levels, block_rows, width = rhs.shape
    return pl.pallas_call(
        last_kernel,
        out_shape=jax.ShapeDtypeStruct((levels, block_rows, width), jnp.float32),
        in_specs=[VMEM] * (3 + len(earlier)),
        out_specs=pl.BlockSpec(memory_space=pl.ANY),
        scratch_shapes=[
            pltpu.VMEM((block_rows, width), jnp.float32),
            pltpu.SemaphoreType.DMA((levels,)),
        ],
        compiler_params=pltpu.CompilerParams(vmem_limit_bytes=KERNEL_VMEM),
        name="solve_last",
    )(*map(in_vmem, (rhs, dinv, arrived, *earlier)))


def on_device(rhs, dinv, lower, sources):
    levels = rhs.shape[0]
    pair_of = {}
    for section in range(levels):
        for target in range(section + 1, levels):
            pair_of[section, target] = len(pair_of)
    rhs, dinv, lower = rhs[:, 0, 0], dinv[:, 0, 0], lower[:, 0, 0]
    sources = jnp.swapaxes(sources[:, 0, 0], 1, 2)
    solution = jnp.dot(
        dinv[0],
        rhs[0].astype(jnp.float32),
        precision=lax.Precision.HIGHEST,
        preferred_element_type=jnp.float32,
    )
    solved = solution.astype(jnp.bfloat16)
    solutions, gathered = [solution], []
    for section in range(1, levels):
        gathered.append(lax.all_gather(solved, "row", axis=0, tiled=False))
        pairs = tuple(pair_of[earlier, section] for earlier in range(section))
        coded = local_terms(pairs, sources, lower, gathered)
        arrived = lax.all_to_all(coded, "col", split_axis=0, concat_axis=0, tiled=True)
        if section + 1 < levels:
            solution, solved = solve_middle(section, rhs, dinv, arrived)
            solutions.append(solution)
        else:
            stacked = solve_last(rhs, dinv, arrived, solutions)
    return stacked[:, None, None]


def solution(mesh):
    in_specs = (
        P(None, "row", "col", None, None),
        P(None, "row", "col", None, None),
        P(None, "row", "col", None, None, None),
        P(None, "row", "col", None, None),
    )
    out_specs = P(None, "row", "col", None, None)
    return jax.shard_map(
        on_device, mesh=mesh, in_specs=in_specs, out_specs=out_specs, check_vma=False
    )
```

```python
import functools

import jax
import jax.numpy as jnp
from jax import lax
from jax.experimental import pallas as pl
from jax.experimental.pallas import tpu as pltpu
from jax.sharding import PartitionSpec as P

LANES = 128
PAD = 8
KERNEL_VMEM = 8 << 20
CHUNKS = 4
VMEM = pl.BlockSpec(memory_space=pltpu.VMEM)


def in_vmem(array):
    return pltpu.with_memory_space_constraint(array, pltpu.VMEM)


def in_hbm(array):
    return pltpu.with_memory_space_constraint(array, pltpu.HBM)


def terms_kernel(pairs, sources_ref, lower_ref, *refs):
    gathered, (out_ref, factors_ref, sems) = refs[:-3], refs[-3:]
    _, targets, block_rows, depth = lower_ref.shape
    chunk = targets // CHUNKS
    copies = [
        [
            pltpu.make_async_copy(
                lower_ref.at[pair, pl.ds(step * chunk, chunk)],
                factors_ref.at[place, pl.ds(step * chunk, chunk)],
                sems.at[step, place],
            )
            for place, pair in enumerate(pairs)
        ]
        for step in range(CHUNKS)
    ]
    for step in range(CHUNKS):
        for copy in copies[step]:
            copy.start()
    per = depth // block_rows

    def one(target, carry):
        factors, picked = [], []
        for place, (block, pair) in enumerate(zip(gathered, pairs)):
            factors.append(factors_ref[place, target])
            for entry in range(per):
                source = sources_ref[pair, entry, target]
                rows = block[jnp.maximum(source, 0)]
                picked.append(jnp.where(source >= 0, rows, jnp.zeros_like(rows)))
        term = jnp.dot(
            jnp.concatenate(factors, axis=1),
            jnp.concatenate(picked, axis=0),
            preferred_element_type=jnp.float32,
        )
        largest = jnp.max(jnp.abs(term), axis=0, keepdims=True)
        power = jnp.ceil(jnp.log2(jnp.maximum(largest * 1.001, 1e-30)))
        coded = jnp.floor(term * jnp.exp2(15.0 - power) + 0.5).astype(jnp.int32)
        out_ref[target, 0:block_rows, :] = coded.astype(jnp.int16)
        powers = jnp.broadcast_to(power, (PAD, LANES)).astype(jnp.int32)
        out_ref[target, block_rows : block_rows + PAD, :] = powers.astype(jnp.int16)
        return carry

    for step in range(CHUNKS):
        for copy in copies[step]:
            copy.wait()
        lax.fori_loop(step * chunk, (step + 1) * chunk, one, 0, unroll=True)


def local_terms(pairs, sources, lower, gathered):
    _, targets, block_rows, depth = lower.shape
    rows = block_rows + PAD
    return pl.pallas_call(
        functools.partial(terms_kernel, pairs),
        out_shape=pltpu.VMEM((targets, rows, LANES), jnp.int16),
        in_specs=[pl.BlockSpec(memory_space=pltpu.SMEM), pl.BlockSpec(memory_space=pl.ANY)]
        + [VMEM] * len(gathered),
        out_specs=VMEM,
        scratch_shapes=[
            pltpu.VMEM((len(pairs), targets, block_rows, depth), lower.dtype),
            pltpu.SemaphoreType.DMA((CHUNKS, len(pairs))),
        ],
        compiler_params=pltpu.CompilerParams(vmem_limit_bytes=KERNEL_VMEM),
        name="local_terms",
    )(in_hbm(sources), in_hbm(lower), *map(in_vmem, gathered))


def solve_level(section, chain, rhs_ref, dinv_ref, arrived_ref):
    peers = arrived_ref.shape[0]
    block_rows = rhs_ref.shape[1]

    def add(peer, total):
        powers = arrived_ref[peer, block_rows : block_rows + PAD, :].astype(jnp.int32)
        scale = jnp.exp2(powers.astype(jnp.float32) - 15.0)[0:1, :]
        coded = arrived_ref[peer, 0:block_rows, :].astype(jnp.int32).astype(jnp.float32)
        return total + coded * scale

    total = lax.fori_loop(0, peers, add, jnp.zeros((block_rows, LANES), jnp.float32), unroll=8)
    columns = rhs_ref[section, :, chain * LANES : (chain + 1) * LANES]
    return jnp.dot(
        dinv_ref[section],
        columns.astype(jnp.float32) - total,
        precision=lax.Precision.HIGHEST,
        preferred_element_type=jnp.float32,
    )


def middle_kernel(section, chain, rhs_ref, dinv_ref, arrived_ref, solution_ref, solved_ref):
    result = solve_level(section, chain, rhs_ref, dinv_ref, arrived_ref)
    solution_ref[...] = result
    solved_ref[...] = result.astype(jnp.bfloat16)


def last_kernel(chain, places, rhs_ref, dinv_ref, arrived_ref, *refs):
    earlier, out_ref, result_ref, sems = refs[:-3], refs[-3], refs[-2], refs[-1]
    section = out_ref.shape[0] - 1
    copies = []
    for index, (place, ref) in enumerate(zip(places, earlier)):
        level, start = place
        target = out_ref.at[level, :, pl.ds(start, ref.shape[1])]
        copies.append(pltpu.make_async_copy(ref, target, sems.at[index]))
    for copy in copies:
        copy.start()
    result_ref[...] = solve_level(section, chain, rhs_ref, dinv_ref, arrived_ref)
    target = out_ref.at[section, :, pl.ds(chain * LANES, LANES)]
    copies.append(pltpu.make_async_copy(result_ref, target, sems.at[len(places)]))
    copies[-1].start()
    for copy in copies:
        copy.wait()


def solve_middle(section, chain, rhs, dinv, arrived):
    block_rows = rhs.shape[1]
    return pl.pallas_call(
        functools.partial(middle_kernel, section, chain),
        out_shape=(
            pltpu.VMEM((block_rows, LANES), jnp.float32),
            pltpu.VMEM((block_rows, LANES), jnp.bfloat16),
        ),
        in_specs=[VMEM] * 3,
        out_specs=(VMEM, VMEM),
        compiler_params=pltpu.CompilerParams(vmem_limit_bytes=KERNEL_VMEM),
        name="solve_middle",
    )(*map(in_vmem, (rhs, dinv, arrived)))


def solve_last(chain, rhs, dinv, arrived, solutions):
    levels, block_rows, width = rhs.shape
    places, earlier = [(0, 0)], [solutions[0][0]]
    for other, results in enumerate(solutions):
        for level, result in enumerate(results[1:], 1):
            places.append((level, other * LANES))
            earlier.append(result)
    return pl.pallas_call(
        functools.partial(last_kernel, chain, tuple(places)),
        out_shape=jax.ShapeDtypeStruct((levels, block_rows, width), jnp.float32),
        in_specs=[VMEM] * (3 + len(earlier)),
        out_specs=pl.BlockSpec(memory_space=pl.ANY),
        scratch_shapes=[
            pltpu.VMEM((block_rows, LANES), jnp.float32),
            pltpu.SemaphoreType.DMA((len(earlier) + 1,)),
        ],
        compiler_params=pltpu.CompilerParams(vmem_limit_bytes=KERNEL_VMEM),
        name="solve_last",
    )(*map(in_vmem, (rhs, dinv, arrived, *earlier)))


def on_device(rhs, dinv, lower, sources):
    levels, _, _, _, width = rhs.shape
    pair_of = {}
    for section in range(levels):
        for target in range(section + 1, levels):
            pair_of[section, target] = len(pair_of)
    rhs, dinv, lower = rhs[:, 0, 0], dinv[:, 0, 0], lower[:, 0, 0]
    sources = jnp.swapaxes(sources[:, 0, 0], 1, 2)
    chains = range(width // LANES)
    first = jnp.dot(
        dinv[0],
        rhs[0].astype(jnp.float32),
        precision=lax.Precision.HIGHEST,
        preferred_element_type=jnp.float32,
    )
    solutions = [[first] for chain in chains]
    solved = [first[:, chain * LANES : (chain + 1) * LANES].astype(jnp.bfloat16) for chain in chains]
    gathered = [[] for chain in chains]
    pending = None
    for section in range(1, levels):
        pairs = tuple(pair_of[earlier, section] for earlier in range(section))
        for chain in chains:
            gathered[chain].append(lax.all_gather(solved[chain], "row", axis=0, tiled=False))
            coded = local_terms(pairs, sources, lower, gathered[chain])
            following = (chain + 1) % len(chains)
            if pending is None:
                coded, solved[following] = lax.optimization_barrier((coded, solved[following]))
            else:
                coded, pending = lax.optimization_barrier((coded, pending))
                before = (chain - 1) % len(chains)
                level = section if before < chain else section - 1
                solution, solved[before] = solve_middle(level, before, rhs, dinv, pending)
                solutions[before].append(solution)
            pending = lax.all_to_all(coded, "col", split_axis=0, concat_axis=0, tiled=True)
    stacked = solve_last(len(chains) - 1, rhs, dinv, pending, solutions)
    return stacked[:, None, None]


def solution(mesh):
    in_specs = (
        P(None, "row", "col", None, None),
        P(None, "row", "col", None, None),
        P(None, "row", "col", None, None, None),
        P(None, "row", "col", None, None),
    )
    out_specs = P(None, "row", "col", None, None)
    return jax.shard_map(
        on_device, mesh=mesh, in_specs=in_specs, out_specs=out_specs, check_vma=False
    )
```

```python
import functools

import jax
import jax.numpy as jnp
from jax import lax
from jax.experimental import pallas as pl
from jax.experimental.pallas import tpu as pltpu
from jax.sharding import Mesh, PartitionSpec as P

LANES = 128
PAD = 8
SIDES = 2
KERNEL_VMEM = 12 << 20
CHUNKS = 4
VMEM = pl.BlockSpec(memory_space=pltpu.VMEM)
SMEM = pl.BlockSpec(memory_space=pltpu.SMEM)
ANY = pl.BlockSpec(memory_space=pl.ANY)
PARAMS = pltpu.CompilerParams(vmem_limit_bytes=KERNEL_VMEM)


def in_vmem(array):
    return pltpu.with_memory_space_constraint(array, pltpu.VMEM)


def in_hbm(array):
    return pltpu.with_memory_space_constraint(array, pltpu.HBM)


def encode(parts, out_ref, index):
    powers = []
    for side, part in enumerate(parts):
        rows = part.shape[0]
        largest = jnp.max(jnp.abs(part), axis=0, keepdims=True)
        power = jnp.ceil(jnp.log2(jnp.maximum(largest * 1.001, 1e-30)))
        coded = jnp.floor(part * jnp.exp2(15.0 - power) + 0.5).astype(jnp.int32)
        out_ref[index, side * rows : (side + 1) * rows, :] = coded.astype(jnp.int16)
        powers.append(jnp.broadcast_to(power, (PAD // len(parts), LANES)))
    powers = jnp.concatenate(powers, axis=0).astype(jnp.int32)
    out_ref[index, len(parts) * rows : len(parts) * rows + PAD, :] = powers.astype(jnp.int16)


def decode(block):
    rows = (block.shape[0] - PAD) // SIDES
    powers = block[SIDES * rows :, :].astype(jnp.int32).astype(jnp.float32)
    scales = jnp.exp2(powers - 15.0)
    parts = []
    for side in range(SIDES):
        coded = block[side * rows : (side + 1) * rows, :].astype(jnp.int32).astype(jnp.float32)
        first = side * (PAD // SIDES)
        parts.append(coded * scales[first : first + 1, :])
    return parts


def add_peers(peers, load):
    total = None
    for peer in range(peers):
        parts = decode(load(peer))
        total = parts if total is None else [a + b for a, b in zip(total, parts)]
    return total


def first_kernel(rhs_ref, dinv_ref, solution_ref, payload_ref):
    solution = jnp.dot(
        dinv_ref[0],
        rhs_ref[0].astype(jnp.float32),
        precision=lax.Precision.HIGHEST,
        preferred_element_type=jnp.float32,
    )
    solution_ref[...] = solution
    for half in range(SIDES):
        columns = slice(half * LANES, (half + 1) * LANES)
        payload_ref[half, 0] = solution[:, columns].astype(jnp.bfloat16)
        for level in range(1, rhs_ref.shape[0]):
            payload_ref[half, level] = rhs_ref[level, :, columns]


def spread_kernel(swapped_ref, copies_ref):
    core = lax.axis_index("core")
    for side, row in enumerate((core, 1 - core)):
        block = swapped_ref[row, 0]
        for peer in range(copies_ref.shape[0]):
            copies_ref[peer, side] = block


def terms_kernel(pairs, *refs):
    sources, lowers, gathered = refs[:SIDES], refs[SIDES : 2 * SIDES], refs[2 * SIDES : -3]
    out_ref, factors_ref, sems = refs[-3:]
    core = lax.axis_index("core")
    _, targets, block_rows, depth = lowers[0].shape
    per = depth // block_rows
    chunk = targets // CHUNKS
    copies = [
        [
            pltpu.make_async_copy(
                lowers[side].at[pair, pl.ds(step * chunk, chunk)],
                factors_ref.at[side, place, pl.ds(step * chunk, chunk)],
                sems.at[step, side, place],
            )
            for side in range(SIDES)
            for place, pair in enumerate(pairs)
        ]
        for step in range(CHUNKS)
    ]
    for step in range(CHUNKS):
        for copy in copies[step]:
            copy.start()

    def one(target, carry):
        parts = []
        for side in range(SIDES):
            factors, picked = [], []
            for place, (block, pair) in enumerate(zip(gathered, pairs)):
                factors.append(factors_ref[side, place, target])
                for entry in range(per):
                    source = sources[side][pair, entry, target]
                    rows = block[jnp.bitwise_xor(jnp.maximum(source, 0), core)]
                    picked.append(jnp.where(source >= 0, rows, jnp.zeros_like(rows)))
            parts.append(
                jnp.dot(
                    jnp.concatenate(factors, axis=1),
                    jnp.concatenate(picked, axis=0),
                    preferred_element_type=jnp.float32,
                )
            )
        encode(parts, out_ref, target)
        return carry

    for step in range(CHUNKS):
        for copy in copies[step]:
            copy.wait()
        lax.fori_loop(step * chunk, (step + 1) * chunk, one, 0, unroll=True)


def middle_kernel(arrived_ref, out_ref):
    peers, targets = arrived_ref.shape[:2]
    for target in range(targets):
        encode(add_peers(peers, lambda peer: arrived_ref[peer, target]), out_ref, target)


def solve_parts(level, swapped_ref, dinv_refs, arrived_ref):
    core = lax.axis_index("core")
    total = add_peers(arrived_ref.shape[0], lambda peer: arrived_ref[peer])
    parts = []
    for row, dinv_ref, part in zip((core, 1 - core), dinv_refs, total):
        residual = swapped_ref[row, level].astype(jnp.float32) - part
        parts.append(
            jnp.dot(
                dinv_ref[level],
                residual,
                precision=lax.Precision.HIGHEST,
                preferred_element_type=jnp.float32,
            )
        )
    return parts


def solve_kernel(level, swapped_ref, own_ref, other_ref, arrived_ref, solution_ref, copies_ref):
    parts = solve_parts(level, swapped_ref, (own_ref, other_ref), arrived_ref)
    for side, part in enumerate(parts):
        solution_ref[side] = part
        for peer in range(copies_ref.shape[0]):
            copies_ref[peer, side] = part.astype(jnp.bfloat16)


def last_kernel(swapped_ref, own_ref, other_ref, arrived_ref, *refs):
    earlier, out_ref = refs[:-1], refs[-1]
    core = lax.axis_index("core")
    for place, ref in enumerate(earlier):
        out_ref[core, place] = ref[0]
        out_ref[1 - core, place] = ref[1]
    level = len(earlier) + 1
    parts = solve_parts(level, swapped_ref, (own_ref, other_ref), arrived_ref)
    out_ref[core, level - 1] = parts[0]
    out_ref[1 - core, level - 1] = parts[1]


def join_kernel(first_ref, halves_ref, out_ref, sems):
    copies = [pltpu.make_async_copy(first_ref, out_ref.at[0], sems.at[0])]
    for half in range(SIDES):
        target = out_ref.at[pl.ds(1, halves_ref.shape[1]), :, pl.ds(half * LANES, LANES)]
        copies.append(pltpu.make_async_copy(halves_ref.at[half], target, sems.at[1 + half]))
    for copy in copies:
        copy.start()
    for copy in copies:
        copy.wait()


def on_device(rhs, dinv, lower, sources):
    levels, _, _, block_rows, width = rhs.shape
    x_size, y_size, z_size = (lax.axis_size(name) for name in ("x", "y", "z"))
    pair_of = {}
    for section in range(levels):
        for target in range(section + 1, levels):
            pair_of[section, target] = len(pair_of)
    rhs, dinv, lower = rhs[:, 0, 0], dinv[:, 0, 0], lower[:, 0, 0]
    sources = jnp.swapaxes(sources[:, 0, 0], 1, 2)
    targets, depth = lower.shape[1], lower.shape[3]
    coded_rows = SIDES * block_rows + PAD
    copies_shape = pltpu.VMEM((y_size, SIDES, block_rows, LANES), jnp.bfloat16)

    first, payload = pl.pallas_call(
        first_kernel,
        out_shape=(
            pltpu.VMEM((block_rows, width), jnp.float32),
            pltpu.VMEM((SIDES, levels, block_rows, LANES), jnp.bfloat16),
        ),
        in_specs=[VMEM] * 2,
        out_specs=(VMEM, VMEM),
        compiler_params=PARAMS,
        name="first",
    )(rhs, dinv)
    swapped = lax.all_to_all(payload, "core", split_axis=0, concat_axis=0, tiled=True)
    copies = pl.pallas_call(
        spread_kernel,
        out_shape=copies_shape,
        in_specs=[VMEM],
        out_specs=VMEM,
        compiler_params=PARAMS,
        name="spread",
    )(in_vmem(swapped))

    swap = [(0, 1), (1, 0)]
    copies, lower_sent, dinv_sent, sources_sent = lax.optimization_barrier(
        (copies, lower, dinv, sources)
    )
    lowers = (lower, lax.ppermute(lower_sent, "core", swap))
    dinvs = (dinv, lax.ppermute(dinv_sent, "core", swap))
    tables = (sources, lax.ppermute(sources_sent, "core", swap))

    gathered, solutions = [], []
    for level in range(1, levels):
        blocks = lax.all_to_all(copies, "y", split_axis=0, concat_axis=0, tiled=True)
        gathered.append(in_vmem(blocks.reshape(y_size * SIDES, block_rows, LANES)))
        pairs = tuple(pair_of[earlier, level] for earlier in range(level))
        coded = pl.pallas_call(
            functools.partial(terms_kernel, pairs),
            out_shape=pltpu.VMEM((targets, coded_rows, LANES), jnp.int16),
            in_specs=[SMEM] * SIDES + [ANY] * SIDES + [VMEM] * len(gathered),
            out_specs=VMEM,
            scratch_shapes=[
                pltpu.VMEM((SIDES, len(pairs), targets, block_rows, depth), lower.dtype),
                pltpu.SemaphoreType.DMA((CHUNKS, SIDES, len(pairs))),
            ],
            compiler_params=PARAMS,
            name="local_terms",
        )(*map(in_hbm, tables), *map(in_hbm, lowers), *gathered)
        coded = coded.reshape(x_size, z_size, coded_rows, LANES)
        arrived = lax.all_to_all(coded, "x", split_axis=0, concat_axis=0, tiled=True)
        coded = pl.pallas_call(
            middle_kernel,
            out_shape=pltpu.VMEM((z_size, coded_rows, LANES), jnp.int16),
            in_specs=[VMEM],
            out_specs=VMEM,
            compiler_params=PARAMS,
            name="sum_x",
        )(in_vmem(arrived))
        arrived = lax.all_to_all(coded, "z", split_axis=0, concat_axis=0, tiled=True)
        operands = [in_vmem(array) for array in (swapped, *dinvs, arrived)]
        if level + 1 < levels:
            solution, copies = pl.pallas_call(
                functools.partial(solve_kernel, level),
                out_shape=(pltpu.VMEM((SIDES, block_rows, LANES), jnp.float32), copies_shape),
                in_specs=[VMEM] * 4,
                out_specs=(VMEM, VMEM),
                compiler_params=PARAMS,
                name="solve",
            )(*operands)
            solutions.append(solution)
        else:
            parts = pl.pallas_call(
                last_kernel,
                out_shape=pltpu.VMEM((SIDES, levels - 1, block_rows, LANES), jnp.float32),
                in_specs=[VMEM] * (4 + len(solutions)),
                out_specs=VMEM,
                compiler_params=PARAMS,
                name="solve_last",
            )(*operands, *map(in_vmem, solutions))
    halves = lax.all_to_all(parts, "core", split_axis=0, concat_axis=0, tiled=True)
    joined = pl.pallas_call(
        join_kernel,
        out_shape=jax.ShapeDtypeStruct((levels, block_rows, width), jnp.float32),
        in_specs=[VMEM] * 2,
        out_specs=ANY,
        scratch_shapes=[pltpu.SemaphoreType.DMA((1 + SIDES,))],
        compiler_params=PARAMS,
        name="join",
    )(in_vmem(first), in_vmem(halves))
    return joined[:, None, None]


def solution(mesh):
    split = Mesh(mesh.devices.reshape(8, 2, 4, 8), ("y", "core", "x", "z"))
    row, col = ("y", "core"), ("x", "z")
    in_specs = (
        P(None, row, col, None, None),
        P(None, row, col, None, None),
        P(None, row, col, None, None, None),
        P(None, row, col, None, None),
    )
    out_specs = P(None, row, col, None, None)
    return jax.shard_map(
        on_device, mesh=split, in_specs=in_specs, out_specs=out_specs, check_vma=False
    )
```

```python
import functools

import jax
import jax.numpy as jnp
from jax import lax
from jax.experimental import pallas as pl
from jax.experimental.pallas import tpu as pltpu
from jax.sharding import Mesh, PartitionSpec as P

LANES = 128
PAD = 8
SIDES = 2
KERNEL_VMEM = 12 << 20
VMEM = pl.BlockSpec(memory_space=pltpu.VMEM)
SMEM = pl.BlockSpec(memory_space=pltpu.SMEM)
ANY = pl.BlockSpec(memory_space=pl.ANY)
PARAMS = pltpu.CompilerParams(vmem_limit_bytes=KERNEL_VMEM)


def in_vmem(array):
    return pltpu.with_memory_space_constraint(array, pltpu.VMEM)


def in_hbm(array):
    return pltpu.with_memory_space_constraint(array, pltpu.HBM)


def encode(parts, out_ref, index):
    powers = []
    for side, part in enumerate(parts):
        rows = part.shape[0]
        largest = jnp.max(jnp.abs(part), axis=0, keepdims=True)
        power = jnp.ceil(jnp.log2(jnp.maximum(largest * 1.001, 1e-30)))
        coded = jnp.floor(part * jnp.exp2(15.0 - power) + 0.5).astype(jnp.int32)
        out_ref[index, side * rows : (side + 1) * rows, :] = coded.astype(jnp.int16)
        powers.append(jnp.broadcast_to(power, (PAD // len(parts), LANES)))
    powers = jnp.concatenate(powers, axis=0).astype(jnp.int32)
    out_ref[index, len(parts) * rows : len(parts) * rows + PAD, :] = powers.astype(jnp.int16)


def decode(block):
    rows = (block.shape[0] - PAD) // SIDES
    powers = block[SIDES * rows :, :].astype(jnp.int32).astype(jnp.float32)
    scales = jnp.exp2(powers - 15.0)
    parts = []
    for side in range(SIDES):
        coded = block[side * rows : (side + 1) * rows, :].astype(jnp.int32).astype(jnp.float32)
        first = side * (PAD // SIDES)
        parts.append(coded * scales[first : first + 1, :])
    return parts


def add_peers(peers, load):
    total = None
    for peer in range(peers):
        parts = decode(load(peer))
        total = parts if total is None else [a + b for a, b in zip(total, parts)]
    return total


def first_kernel(rhs_hbm, dinv_hbm, sources_ref, solution_ref, mine_ref, sent_ref, rhs_ref, dinv_ref, sems):
    copies = [
        pltpu.make_async_copy(rhs_hbm, rhs_ref, sems.at[0]),
        pltpu.make_async_copy(dinv_hbm, dinv_ref, sems.at[1]),
    ]
    for copy in copies:
        copy.start()
    levels, block_rows, _ = rhs_ref.shape
    base = levels * block_rows
    sent_ref[base:, :] = jnp.zeros((sent_ref.shape[0] - base, LANES), jnp.float32)
    tables = base + (levels - 1) * block_rows
    pairs, per, targets = sources_ref.shape
    for pair in range(pairs):
        rows = slice(tables + pair * per, tables + (pair + 1) * per)
        sent_ref[rows, 0:targets] = sources_ref[pair].astype(jnp.float32)
    for copy in copies:
        copy.wait()
    solution = jnp.dot(
        dinv_ref[0],
        rhs_ref[0].astype(jnp.float32),
        precision=lax.Precision.HIGHEST,
        preferred_element_type=jnp.float32,
    )
    solution_ref[...] = solution
    left_is_mine = lax.axis_index("core") == 0
    for level in range(levels):
        block = rhs_ref[level].astype(jnp.float32) if level else solution
        left, right = block[:, :LANES], block[:, LANES:]
        mine_ref[level] = jnp.where(left_is_mine, left, right).astype(jnp.bfloat16)
        rows = slice(level * block_rows, (level + 1) * block_rows)
        sent_ref[rows, :] = jnp.where(left_is_mine, right, left)
        if level:
            rows = slice(base + (level - 1) * block_rows, base + level * block_rows)
            sent_ref[rows, 0:block_rows] = dinv_ref[level]


def spread_kernel(mine_ref, swapped_ref, copies_ref, table_ref):
    block_rows = mine_ref.shape[1]
    other = swapped_ref.at[1 - lax.axis_index("core")]
    blocks = mine_ref[0], other[0:block_rows, :].astype(jnp.bfloat16)
    for side, block in enumerate(blocks):
        for peer in range(copies_ref.shape[0]):
            copies_ref[peer, side] = block
    rows = table_ref.shape[0]
    table_ref[...] = other[other.shape[0] - rows :, :].astype(jnp.int32)


def terms_kernel(pairs, own_table, other_table, *refs):
    lowers, gathered, out_ref = refs[:SIDES], refs[SIDES:-1], refs[-1]
    core = lax.axis_index("core")
    _, targets, block_rows, depth = lowers[0].shape
    per = depth // block_rows

    def one(target, carry):
        parts = []
        for side in range(SIDES):
            factors, picked = [], []
            for block, pair in zip(gathered, pairs):
                factors.append(lowers[side][pair, target])
                for entry in range(per):
                    if side == 0:
                        source = own_table[pair, entry, target]
                    else:
                        source = other_table[pair * per + entry, target]
                    rows = block[jnp.bitwise_xor(jnp.maximum(source, 0), core)]
                    picked.append(jnp.where(source >= 0, rows, jnp.zeros_like(rows)))
            parts.append(
                jnp.dot(
                    jnp.concatenate(factors, axis=1),
                    jnp.concatenate(picked, axis=0),
                    preferred_element_type=jnp.float32,
                )
            )
        encode(parts, out_ref, target)
        return carry

    lax.fori_loop(0, targets, one, 0, unroll=8)


def middle_kernel(arrived_ref, out_ref):
    peers, targets = arrived_ref.shape[:2]
    for target in range(targets):
        encode(add_peers(peers, lambda peer: arrived_ref[peer, target]), out_ref, target)


def solve_parts(level, mine_ref, swapped_ref, dinv_ref, arrived_ref):
    levels, block_rows, _ = mine_ref.shape
    other = swapped_ref.at[1 - lax.axis_index("core")]
    base = (levels + level - 1) * block_rows
    blocks = mine_ref[level].astype(jnp.float32), other[level * block_rows : (level + 1) * block_rows, :]
    factors = dinv_ref[level], other[base : base + block_rows, 0:block_rows]
    total = add_peers(arrived_ref.shape[0], lambda peer: arrived_ref[peer])
    return [
        jnp.dot(
            factor,
            block - part,
            precision=lax.Precision.HIGHEST,
            preferred_element_type=jnp.float32,
        )
        for factor, block, part in zip(factors, blocks, total)
    ]


def solve_kernel(level, mine_ref, swapped_ref, dinv_ref, arrived_ref, solution_ref, copies_ref):
    parts = solve_parts(level, mine_ref, swapped_ref, dinv_ref, arrived_ref)
    for side, part in enumerate(parts):
        solution_ref[side] = part
        for peer in range(copies_ref.shape[0]):
            copies_ref[peer, side] = part.astype(jnp.bfloat16)


def last_kernel(mine_ref, swapped_ref, dinv_ref, arrived_ref, *refs):
    earlier, outs = refs[:-SIDES], refs[-SIDES:]
    for place, ref in enumerate(earlier):
        for side, out_ref in enumerate(outs):
            out_ref[place] = ref[side]
    level = len(earlier) + 1
    parts = solve_parts(level, mine_ref, swapped_ref, dinv_ref, arrived_ref)
    for part, out_ref in zip(parts, outs):
        out_ref[level - 1] = part


def join_kernel(first_ref, mine_ref, swapped_ref, out_ref, sems):
    core = lax.axis_index("core")
    later = pl.ds(1, mine_ref.shape[0])
    copies = [pltpu.make_async_copy(first_ref, out_ref.at[0], sems.at[0])]
    for index, (half, ref) in enumerate(((core, mine_ref), (1 - core, swapped_ref.at[1 - core]))):
        columns = pl.ds(pl.multiple_of(half * LANES, LANES), LANES)
        copies.append(pltpu.make_async_copy(ref, out_ref.at[later, :, columns], sems.at[1 + index]))
    for copy in copies:
        copy.start()
    for copy in copies:
        copy.wait()


def on_device(rhs, dinv, lower, sources):
    levels, _, _, block_rows, width = rhs.shape
    x_size, y_size, z_size = (lax.axis_size(name) for name in ("x", "y", "z"))
    pair_of = {}
    for section in range(levels):
        for target in range(section + 1, levels):
            pair_of[section, target] = len(pair_of)
    rhs, dinv, lower = rhs[:, 0, 0], dinv[:, 0, 0], lower[:, 0, 0]
    sources = jnp.swapaxes(sources[:, 0, 0], 1, 2)
    targets = lower.shape[1]
    coded_rows = SIDES * block_rows + PAD
    copies_shape = pltpu.VMEM((y_size, SIDES, block_rows, LANES), jnp.bfloat16)

    table_rows = -(-sources.shape[0] * sources.shape[1] // PAD) * PAD
    sent_rows = (2 * levels - 1) * block_rows + table_rows
    first, mine, sent = pl.pallas_call(
        first_kernel,
        out_shape=(
            pltpu.VMEM((block_rows, width), jnp.float32),
            pltpu.VMEM((levels, block_rows, LANES), jnp.bfloat16),
            pltpu.VMEM((sent_rows, LANES), jnp.float32),
        ),
        in_specs=[ANY, ANY, VMEM],
        out_specs=(VMEM,) * 3,
        scratch_shapes=[
            pltpu.VMEM(rhs.shape, rhs.dtype),
            pltpu.VMEM(dinv.shape, dinv.dtype),
            pltpu.SemaphoreType.DMA((2,)),
        ],
        compiler_params=PARAMS,
        name="first",
    )(in_hbm(rhs), in_hbm(dinv), in_hbm(sources))
    swapped = in_vmem(lax.all_gather(sent, "core", axis=0, tiled=False))
    mine = in_vmem(mine)
    copies, table = pl.pallas_call(
        spread_kernel,
        out_shape=(copies_shape, pltpu.VMEM((table_rows, LANES), jnp.int32)),
        in_specs=[VMEM] * 2,
        out_specs=(VMEM, VMEM),
        compiler_params=PARAMS,
        name="spread",
    )(mine, swapped)
    copies, lower_sent = lax.optimization_barrier((copies, lower))
    lowers = (lower, lax.ppermute(lower_sent, "core", [(0, 1), (1, 0)]))

    gathered, solutions = [], []
    for level in range(1, levels):
        blocks = lax.all_to_all(copies, "y", split_axis=0, concat_axis=0, tiled=True)
        gathered.append(in_vmem(blocks.reshape(y_size * SIDES, block_rows, LANES)))
        pairs = tuple(pair_of[earlier, level] for earlier in range(level))
        coded = pl.pallas_call(
            functools.partial(terms_kernel, pairs),
            out_shape=pltpu.VMEM((targets, coded_rows, LANES), jnp.int16),
            in_specs=[SMEM] * 2 + [VMEM] * (SIDES + len(gathered)),
            out_specs=VMEM,
            compiler_params=PARAMS,
            name="local_terms",
        )(in_hbm(sources), table, *map(in_vmem, lowers), *gathered)
        coded = coded.reshape(x_size, z_size, coded_rows, LANES)
        arrived = lax.all_to_all(coded, "x", split_axis=0, concat_axis=0, tiled=True)
        coded = pl.pallas_call(
            middle_kernel,
            out_shape=pltpu.VMEM((z_size, coded_rows, LANES), jnp.int16),
            in_specs=[VMEM],
            out_specs=VMEM,
            compiler_params=PARAMS,
            name="sum_x",
        )(in_vmem(arrived))
        arrived = lax.all_to_all(coded, "z", split_axis=0, concat_axis=0, tiled=True)
        operands = [mine, swapped] + [in_vmem(array) for array in (dinv, arrived)]
        if level + 1 < levels:
            solution, copies = pl.pallas_call(
                functools.partial(solve_kernel, level),
                out_shape=(pltpu.VMEM((SIDES, block_rows, LANES), jnp.float32), copies_shape),
                in_specs=[VMEM] * 4,
                out_specs=(VMEM, VMEM),
                compiler_params=PARAMS,
                name="solve",
            )(*operands)
            solutions.append(solution)
        else:
            parts = pl.pallas_call(
                last_kernel,
                out_shape=(pltpu.VMEM((levels - 1, block_rows, LANES), jnp.float32),) * SIDES,
                in_specs=[VMEM] * (4 + len(solutions)),
                out_specs=(VMEM,) * SIDES,
                compiler_params=PARAMS,
                name="solve_last",
            )(*operands, *map(in_vmem, solutions))
    halves = lax.all_gather(parts[1], "core", axis=0, tiled=False)
    joined = pl.pallas_call(
        join_kernel,
        out_shape=jax.ShapeDtypeStruct((levels, block_rows, width), jnp.float32),
        in_specs=[VMEM] * 3,
        out_specs=ANY,
        scratch_shapes=[pltpu.SemaphoreType.DMA((1 + SIDES,))],
        compiler_params=PARAMS,
        name="join",
    )(in_vmem(first), in_vmem(parts[0]), in_vmem(halves))
    return joined[:, None, None]


def solution(mesh):
    split = Mesh(mesh.devices.reshape(8, 2, 4, 8), ("y", "core", "x", "z"))
    row, col = ("y", "core"), ("x", "z")
    in_specs = (
        P(None, row, col, None, None),
        P(None, row, col, None, None),
        P(None, row, col, None, None, None),
        P(None, row, col, None, None),
    )
    out_specs = P(None, row, col, None, None)
    return jax.shard_map(
        on_device, mesh=split, in_specs=in_specs, out_specs=out_specs, check_vma=False
    )
```

```python
import functools

import jax
import jax.numpy as jnp
from jax import lax
from jax.experimental import pallas as pl
from jax.experimental.pallas import tpu as pltpu
from jax.sharding import Mesh, PartitionSpec as P

LANES = 128
PAD = 8
SIDES = 2
KERNEL_VMEM = 12 << 20
VMEM = pl.BlockSpec(memory_space=pltpu.VMEM)
SMEM = pl.BlockSpec(memory_space=pltpu.SMEM)
ANY = pl.BlockSpec(memory_space=pl.ANY)
PARAMS = pltpu.CompilerParams(vmem_limit_bytes=KERNEL_VMEM)


def in_vmem(array):
    return pltpu.with_memory_space_constraint(array, pltpu.VMEM)


def in_hbm(array):
    return pltpu.with_memory_space_constraint(array, pltpu.HBM)


def encode(parts, out_ref, index):
    powers = []
    for side, part in enumerate(parts):
        rows = part.shape[0]
        largest = jnp.max(jnp.abs(part), axis=0, keepdims=True)
        power = jnp.ceil(jnp.log2(jnp.maximum(largest * 1.001, 1e-30)))
        coded = jnp.floor(part * jnp.exp2(15.0 - power) + 0.5).astype(jnp.int32)
        out_ref[index, side * rows : (side + 1) * rows, :] = coded.astype(jnp.int16)
        powers.append(jnp.broadcast_to(power, (PAD // len(parts), LANES)))
    powers = jnp.concatenate(powers, axis=0).astype(jnp.int32)
    out_ref[index, len(parts) * rows : len(parts) * rows + PAD, :] = powers.astype(jnp.int16)


def decode(block):
    rows = (block.shape[0] - PAD) // SIDES
    powers = block[SIDES * rows :, :].astype(jnp.int32).astype(jnp.float32)
    scales = jnp.exp2(powers - 15.0)
    parts = []
    for side in range(SIDES):
        coded = block[side * rows : (side + 1) * rows, :].astype(jnp.int32).astype(jnp.float32)
        first = side * (PAD // SIDES)
        parts.append(coded * scales[first : first + 1, :])
    return parts


def add_peers(peers, load):
    total = None
    for peer in range(peers):
        parts = decode(load(peer))
        total = parts if total is None else [a + b for a, b in zip(total, parts)]
    return total


def first_kernel(rhs_hbm, dinv_hbm, lower_hbm, sources_ref, *refs):
    solution_ref, mine_ref, sent_ref, factors_ref, rhs_ref, dinv_ref, sems = refs
    copies = [
        pltpu.make_async_copy(rhs_hbm, rhs_ref, sems.at[0]),
        pltpu.make_async_copy(dinv_hbm, dinv_ref, sems.at[1]),
    ]
    early = pltpu.make_async_copy(
        lower_hbm.at[pl.ds(0, factors_ref.shape[0])], factors_ref, sems.at[2]
    )
    for copy in (*copies, early):
        copy.start()
    levels, block_rows, _ = rhs_ref.shape
    base = levels * block_rows
    sent_ref[base:, :] = jnp.zeros((sent_ref.shape[0] - base, LANES), jnp.float32)
    tables = base + (levels - 1) * block_rows
    pairs, per, targets = sources_ref.shape
    for pair in range(pairs):
        rows = slice(tables + pair * per, tables + (pair + 1) * per)
        sent_ref[rows, 0:targets] = sources_ref[pair].astype(jnp.float32)
    for copy in copies:
        copy.wait()
    solution = jnp.dot(
        dinv_ref[0],
        rhs_ref[0].astype(jnp.float32),
        precision=lax.Precision.HIGHEST,
        preferred_element_type=jnp.float32,
    )
    solution_ref[...] = solution
    left_is_mine = lax.axis_index("core") == 0
    for level in range(levels):
        block = rhs_ref[level].astype(jnp.float32) if level else solution
        left, right = block[:, :LANES], block[:, LANES:]
        mine_ref[level] = jnp.where(left_is_mine, left, right).astype(jnp.bfloat16)
        rows = slice(level * block_rows, (level + 1) * block_rows)
        sent_ref[rows, :] = jnp.where(left_is_mine, right, left)
        if level:
            rows = slice(base + (level - 1) * block_rows, base + level * block_rows)
            sent_ref[rows, 0:block_rows] = dinv_ref[level]
    early.wait()


def spread_kernel(mine_ref, swapped_ref, copies_ref, table_ref):
    block_rows = mine_ref.shape[1]
    other = swapped_ref.at[1 - lax.axis_index("core")]
    blocks = mine_ref[0], other[0:block_rows, :].astype(jnp.bfloat16)
    for side, block in enumerate(blocks):
        for peer in range(copies_ref.shape[0]):
            copies_ref[peer, side] = block
    rows = table_ref.shape[0]
    table_ref[...] = other[other.shape[0] - rows :, :].astype(jnp.int32)


def terms_kernel(pairs, z_sizes, own_table, other_table, *refs):
    lowers, gathered, out_ref = refs[:SIDES], refs[SIDES:-1], refs[-1]
    core = lax.axis_index("core")
    _, targets, block_rows, depth = lowers[0].shape
    per = depth // block_rows
    za_size, zb_size = z_sizes
    z_size = za_size * zb_size

    def one(target, carry):
        z = lax.rem(target, z_size)
        slot = target - z + lax.rem(z, zb_size) * za_size + lax.div(z, zb_size)
        parts = []
        for side in range(SIDES):
            factors, picked = [], []
            for block, pair in zip(gathered, pairs):
                factors.append(lowers[side][pair, target])
                for entry in range(per):
                    if side == 0:
                        source = own_table[pair, entry, target]
                    else:
                        source = other_table[pair * per + entry, target]
                    rows = block[jnp.bitwise_xor(jnp.maximum(source, 0), core)]
                    picked.append(jnp.where(source >= 0, rows, jnp.zeros_like(rows)))
            parts.append(
                jnp.dot(
                    jnp.concatenate(factors, axis=1),
                    jnp.concatenate(picked, axis=0),
                    preferred_element_type=jnp.float32,
                )
            )
        encode(parts, out_ref, slot)
        return carry

    lax.fori_loop(0, targets, one, 0, unroll=8)


def middle_kernel(arrived_ref, out_ref):
    peers, targets = arrived_ref.shape[:2]
    for target in range(targets):
        encode(add_peers(peers, lambda peer: arrived_ref[peer, target]), out_ref, target)


def solve_parts(level, mine_ref, swapped_ref, dinv_ref, arrived_ref):
    levels, block_rows, _ = mine_ref.shape
    other = swapped_ref.at[1 - lax.axis_index("core")]
    base = (levels + level - 1) * block_rows
    blocks = mine_ref[level].astype(jnp.float32), other[level * block_rows : (level + 1) * block_rows, :]
    factors = dinv_ref[level], other[base : base + block_rows, 0:block_rows]
    total = add_peers(arrived_ref.shape[0], lambda peer: arrived_ref[peer])
    return [
        jnp.dot(
            factor,
            block - part,
            precision=lax.Precision.HIGHEST,
            preferred_element_type=jnp.float32,
        )
        for factor, block, part in zip(factors, blocks, total)
    ]


def solve_kernel(level, mine_ref, swapped_ref, dinv_ref, arrived_ref, solution_ref, copies_ref):
    parts = solve_parts(level, mine_ref, swapped_ref, dinv_ref, arrived_ref)
    for side, part in enumerate(parts):
        solution_ref[side] = part
        for peer in range(copies_ref.shape[0]):
            copies_ref[peer, side] = part.astype(jnp.bfloat16)


def last_kernel(mine_ref, swapped_ref, dinv_ref, arrived_ref, *refs):
    earlier, outs = refs[:-SIDES], refs[-SIDES:]
    for place, ref in enumerate(earlier):
        for side, out_ref in enumerate(outs):
            out_ref[place] = ref[side]
    level = len(earlier) + 1
    parts = solve_parts(level, mine_ref, swapped_ref, dinv_ref, arrived_ref)
    for part, out_ref in zip(parts, outs):
        out_ref[level - 1] = part


def join_kernel(first_ref, mine_ref, swapped_ref, out_ref, sems):
    core = lax.axis_index("core")
    later = pl.ds(1, mine_ref.shape[0])
    copies = [pltpu.make_async_copy(first_ref, out_ref.at[0], sems.at[0])]
    for index, (half, ref) in enumerate(((core, mine_ref), (1 - core, swapped_ref.at[1 - core]))):
        columns = pl.ds(pl.multiple_of(half * LANES, LANES), LANES)
        copies.append(pltpu.make_async_copy(ref, out_ref.at[later, :, columns], sems.at[1 + index]))
    for copy in copies:
        copy.start()
    for copy in copies:
        copy.wait()


def on_device(rhs, dinv, lower, sources):
    levels, _, _, block_rows, width = rhs.shape
    y_size, x_size, za_size, zb_size = (lax.axis_size(name) for name in ("y", "x", "za", "zb"))
    pair_of = {}
    for section in range(levels):
        for target in range(section + 1, levels):
            pair_of[section, target] = len(pair_of)
    rhs, dinv, lower = rhs[:, 0, 0], dinv[:, 0, 0], lower[:, 0, 0]
    sources = jnp.swapaxes(sources[:, 0, 0], 1, 2)
    targets = lower.shape[1]
    coded_rows = SIDES * block_rows + PAD
    copies_shape = pltpu.VMEM((y_size, SIDES, block_rows, LANES), jnp.bfloat16)

    table_rows = -(-sources.shape[0] * sources.shape[1] // PAD) * PAD
    sent_rows = (2 * levels - 1) * block_rows + table_rows
    first, mine, sent, early = pl.pallas_call(
        first_kernel,
        out_shape=(
            pltpu.VMEM((block_rows, width), jnp.float32),
            pltpu.VMEM((levels, block_rows, LANES), jnp.bfloat16),
            pltpu.VMEM((sent_rows, LANES), jnp.float32),
            pltpu.VMEM((1,) + lower.shape[1:], lower.dtype),
        ),
        in_specs=[ANY, ANY, ANY, VMEM],
        out_specs=(VMEM,) * 4,
        scratch_shapes=[
            pltpu.VMEM(rhs.shape, rhs.dtype),
            pltpu.VMEM(dinv.shape, dinv.dtype),
            pltpu.SemaphoreType.DMA((3,)),
        ],
        compiler_params=PARAMS,
        name="first",
    )(in_hbm(rhs), in_hbm(dinv), in_hbm(lower), in_hbm(sources))
    swapped = in_vmem(lax.all_gather(sent, "core", axis=0, tiled=False))
    mine = in_vmem(mine)
    copies, table = pl.pallas_call(
        spread_kernel,
        out_shape=(copies_shape, pltpu.VMEM((table_rows, LANES), jnp.int32)),
        in_specs=[VMEM] * 2,
        out_specs=(VMEM, VMEM),
        compiler_params=PARAMS,
        name="spread",
    )(mine, swapped)
    copies, lower_sent = lax.optimization_barrier((copies, lower))
    other_lower = lax.ppermute(lower_sent, "core", [(0, 1), (1, 0)])

    gathered, solutions = [], []
    for level in range(1, levels):
        blocks = lax.all_to_all(copies, "y", split_axis=0, concat_axis=0, tiled=True)
        gathered.append(in_vmem(blocks.reshape(y_size * SIDES, block_rows, LANES)))
        pairs = tuple(pair_of[earlier, level] for earlier in range(level))
        own = early if level == 1 else lower
        coded = pl.pallas_call(
            functools.partial(terms_kernel, pairs, (za_size, zb_size)),
            out_shape=pltpu.VMEM((targets, coded_rows, LANES), jnp.int16),
            in_specs=[SMEM] * 2 + [VMEM] * (SIDES + len(gathered)),
            out_specs=VMEM,
            compiler_params=PARAMS,
            name="local_terms",
        )(in_hbm(sources), table, in_vmem(own), in_vmem(other_lower), *gathered)
        coded = coded.reshape(x_size * zb_size, za_size, coded_rows, LANES)
        arrived = lax.all_to_all(coded, ("x", "zb"), split_axis=0, concat_axis=0, tiled=True)
        coded = pl.pallas_call(
            middle_kernel,
            out_shape=pltpu.VMEM((za_size, coded_rows, LANES), jnp.int16),
            in_specs=[VMEM],
            out_specs=VMEM,
            compiler_params=PARAMS,
            name="sum_near",
        )(in_vmem(arrived))
        arrived = lax.all_to_all(coded, "za", split_axis=0, concat_axis=0, tiled=True)
        operands = [mine, swapped] + [in_vmem(array) for array in (dinv, arrived)]
        if level + 1 < levels:
            solution, copies = pl.pallas_call(
                functools.partial(solve_kernel, level),
                out_shape=(pltpu.VMEM((SIDES, block_rows, LANES), jnp.float32), copies_shape),
                in_specs=[VMEM] * 4,
                out_specs=(VMEM, VMEM),
                compiler_params=PARAMS,
                name="solve",
            )(*operands)
            solutions.append(solution)
        else:
            parts = pl.pallas_call(
                last_kernel,
                out_shape=(pltpu.VMEM((levels - 1, block_rows, LANES), jnp.float32),) * SIDES,
                in_specs=[VMEM] * (4 + len(solutions)),
                out_specs=(VMEM,) * SIDES,
                compiler_params=PARAMS,
                name="solve_last",
            )(*operands, *map(in_vmem, solutions))
    halves = lax.all_gather(parts[1], "core", axis=0, tiled=False)
    joined = pl.pallas_call(
        join_kernel,
        out_shape=jax.ShapeDtypeStruct((levels, block_rows, width), jnp.float32),
        in_specs=[VMEM] * 3,
        out_specs=ANY,
        scratch_shapes=[pltpu.SemaphoreType.DMA((1 + SIDES,))],
        compiler_params=PARAMS,
        name="join",
    )(in_vmem(first), in_vmem(parts[0]), in_vmem(halves))
    return joined[:, None, None]


def solution(mesh):
    split = Mesh(mesh.devices.reshape(8, 2, 4, 4, 2), ("y", "core", "x", "za", "zb"))
    row, col = ("y", "core"), ("x", "za", "zb")
    in_specs = (
        P(None, row, col, None, None),
        P(None, row, col, None, None),
        P(None, row, col, None, None, None),
        P(None, row, col, None, None),
    )
    out_specs = P(None, row, col, None, None)
    return jax.shard_map(
        on_device, mesh=split, in_specs=in_specs, out_specs=out_specs, check_vma=False
    )
```

```python
import functools

import jax
import jax.numpy as jnp
from jax import lax
from jax.experimental import pallas as pl
from jax.experimental.pallas import tpu as pltpu
from jax.sharding import Mesh, PartitionSpec as P

LANES = 128
PAD = 8
SIDES = 2
KERNEL_VMEM = 12 << 20
VMEM = pl.BlockSpec(memory_space=pltpu.VMEM)
SMEM = pl.BlockSpec(memory_space=pltpu.SMEM)
ANY = pl.BlockSpec(memory_space=pl.ANY)
PARAMS = pltpu.CompilerParams(vmem_limit_bytes=KERNEL_VMEM)


def in_vmem(array):
    return pltpu.with_memory_space_constraint(array, pltpu.VMEM)


def in_hbm(array):
    return pltpu.with_memory_space_constraint(array, pltpu.HBM)


def encode(parts, out_ref, index):
    powers = []
    for side, part in enumerate(parts):
        rows = part.shape[0]
        largest = jnp.max(jnp.abs(part), axis=0, keepdims=True)
        power = jnp.ceil(jnp.log2(jnp.maximum(largest * 1.001, 1e-30)))
        coded = jnp.round(part * jnp.exp2(15.0 - power)).astype(jnp.int32)
        out_ref[index, side * rows : (side + 1) * rows, :] = coded.astype(jnp.int16)
        powers.append(jnp.broadcast_to(power, (PAD // len(parts), LANES)))
    powers = jnp.concatenate(powers, axis=0).astype(jnp.int32)
    out_ref[index, len(parts) * rows : len(parts) * rows + PAD, :] = powers.astype(jnp.int16)


def decode(block):
    rows = (block.shape[0] - PAD) // SIDES
    powers = block[SIDES * rows :, :].astype(jnp.int32).astype(jnp.float32)
    scales = jnp.exp2(powers - 15.0)
    parts = []
    for side in range(SIDES):
        coded = block[side * rows : (side + 1) * rows, :].astype(jnp.int32).astype(jnp.float32)
        first = side * (PAD // SIDES)
        parts.append(coded * scales[first : first + 1, :])
    return parts


def add_peers(peers, load):
    total = None
    for peer in range(peers):
        parts = decode(load(peer))
        total = parts if total is None else [a + b for a, b in zip(total, parts)]
    return total


def first_kernel(rhs_hbm, dinv_hbm, lower_hbm, sources_ref, *refs):
    solution_ref, mine_ref, sent_ref, factors_ref, rhs_ref, dinv_ref, sems = refs
    copies = [
        pltpu.make_async_copy(rhs_hbm, rhs_ref, sems.at[0]),
        pltpu.make_async_copy(dinv_hbm, dinv_ref, sems.at[1]),
    ]
    early = pltpu.make_async_copy(
        lower_hbm.at[pl.ds(0, factors_ref.shape[0])], factors_ref, sems.at[2]
    )
    for copy in (*copies, early):
        copy.start()
    levels, block_rows, _ = rhs_ref.shape
    base = levels * block_rows
    sent_ref[base:, :] = jnp.zeros((sent_ref.shape[0] - base, LANES), jnp.float32)
    tables = base + (levels - 1) * block_rows
    pairs, per, targets = sources_ref.shape
    for pair in range(pairs):
        rows = slice(tables + pair * per, tables + (pair + 1) * per)
        sent_ref[rows, 0:targets] = sources_ref[pair].astype(jnp.float32)
    for copy in copies:
        copy.wait()
    solution = jnp.dot(
        dinv_ref[0],
        rhs_ref[0].astype(jnp.float32),
        precision=lax.Precision.HIGHEST,
        preferred_element_type=jnp.float32,
    )
    solution_ref[...] = solution
    left_is_mine = lax.axis_index("core") == 0
    for level in range(levels):
        block = rhs_ref[level].astype(jnp.float32) if level else solution
        left, right = block[:, :LANES], block[:, LANES:]
        mine_ref[level] = jnp.where(left_is_mine, left, right).astype(jnp.bfloat16)
        rows = slice(level * block_rows, (level + 1) * block_rows)
        sent_ref[rows, :] = jnp.where(left_is_mine, right, left)
        if level:
            rows = slice(base + (level - 1) * block_rows, base + level * block_rows)
            sent_ref[rows, 0:block_rows] = dinv_ref[level]
    early.wait()


def spread_kernel(mine_ref, swapped_ref, sources_ref, copies_ref, table_ref):
    core = lax.axis_index("core")
    block_rows = mine_ref.shape[1]
    other = swapped_ref.at[1 - core]
    blocks = mine_ref[0], other[0:block_rows, :].astype(jnp.bfloat16)
    for side, block in enumerate(blocks):
        for peer in range(copies_ref.shape[0]):
            copies_ref[peer, side] = block
    none = SIDES * copies_ref.shape[0]

    def places(sources):
        return jnp.where(sources >= 0, jnp.bitwise_xor(sources, core), none)

    pairs, per, targets = sources_ref.shape
    rows = table_ref.shape[1]
    table_ref[0] = jnp.zeros(table_ref.shape[1:], jnp.int32)
    for pair in range(pairs):
        table_ref[0, pair * per : (pair + 1) * per, 0:targets] = places(sources_ref[pair])
    table_ref[1] = places(other[other.shape[0] - rows :, :].astype(jnp.int32))


def terms_kernel(pairs, z_sizes, table_ref, *refs):
    lowers, gathered, (out_ref, blocks_ref) = refs[:SIDES], refs[SIDES:-2], refs[-2:]
    _, targets, block_rows, depth = lowers[0].shape
    per = depth // block_rows
    za_size, zb_size = z_sizes
    z_size = za_size * zb_size
    none = blocks_ref.shape[1] - 1
    for place, block in enumerate(gathered):
        blocks_ref[place, 0:none] = block[...]
        blocks_ref[place, none] = jnp.zeros(blocks_ref.shape[2:], blocks_ref.dtype)

    def one(target, carry):
        z = lax.rem(target, z_size)
        slot = target - z + lax.rem(z, zb_size) * za_size + lax.div(z, zb_size)
        parts = []
        for side in range(SIDES):
            factors, picked = [], []
            for place, pair in enumerate(pairs):
                factors.append(lowers[side][pair, target])
                for entry in range(per):
                    picked.append(blocks_ref[place, table_ref[side, pair * per + entry, target]])
            parts.append(
                jnp.dot(
                    jnp.concatenate(factors, axis=1),
                    jnp.concatenate(picked, axis=0),
                    preferred_element_type=jnp.float32,
                )
            )
        encode(parts, out_ref, slot)
        return carry

    lax.fori_loop(0, targets, one, 0, unroll=True)


def middle_kernel(arrived_ref, out_ref):
    peers, targets = arrived_ref.shape[:2]
    for target in range(targets):
        encode(add_peers(peers, lambda peer: arrived_ref[peer, target]), out_ref, target)


def solve_parts(level, mine_ref, swapped_ref, dinv_ref, arrived_ref):
    levels, block_rows, _ = mine_ref.shape
    other = swapped_ref.at[1 - lax.axis_index("core")]
    base = (levels + level - 1) * block_rows
    blocks = mine_ref[level].astype(jnp.float32), other[level * block_rows : (level + 1) * block_rows, :]
    factors = dinv_ref[level], other[base : base + block_rows, 0:block_rows]
    total = add_peers(arrived_ref.shape[0], lambda peer: arrived_ref[peer])
    return [
        jnp.dot(
            factor,
            block - part,
            precision=lax.Precision.HIGHEST,
            preferred_element_type=jnp.float32,
        )
        for factor, block, part in zip(factors, blocks, total)
    ]


def solve_kernel(level, mine_ref, swapped_ref, dinv_ref, arrived_ref, solution_ref, copies_ref):
    parts = solve_parts(level, mine_ref, swapped_ref, dinv_ref, arrived_ref)
    for side, part in enumerate(parts):
        solution_ref[side] = part
        for peer in range(copies_ref.shape[0]):
            copies_ref[peer, side] = part.astype(jnp.bfloat16)


def last_kernel(mine_ref, swapped_ref, dinv_ref, arrived_ref, *refs):
    earlier, outs = refs[:-SIDES], refs[-SIDES:]
    for place, ref in enumerate(earlier):
        for side, out_ref in enumerate(outs):
            out_ref[place] = ref[side]
    level = len(earlier) + 1
    parts = solve_parts(level, mine_ref, swapped_ref, dinv_ref, arrived_ref)
    for part, out_ref in zip(parts, outs):
        out_ref[level - 1] = part


def join_kernel(first_ref, mine_ref, swapped_ref, out_ref, sems):
    core = lax.axis_index("core")
    later = pl.ds(1, mine_ref.shape[0])
    copies = [pltpu.make_async_copy(first_ref, out_ref.at[0], sems.at[0])]
    for index, (half, ref) in enumerate(((core, mine_ref), (1 - core, swapped_ref.at[1 - core]))):
        columns = pl.ds(pl.multiple_of(half * LANES, LANES), LANES)
        copies.append(pltpu.make_async_copy(ref, out_ref.at[later, :, columns], sems.at[1 + index]))
    for copy in copies:
        copy.start()
    for copy in copies:
        copy.wait()


def on_device(rhs, dinv, lower, sources):
    levels, _, _, block_rows, width = rhs.shape
    y_size, x_size, za_size, zb_size = (lax.axis_size(name) for name in ("y", "x", "za", "zb"))
    pair_of = {}
    for section in range(levels):
        for target in range(section + 1, levels):
            pair_of[section, target] = len(pair_of)
    rhs, dinv, lower = rhs[:, 0, 0], dinv[:, 0, 0], lower[:, 0, 0]
    sources = jnp.swapaxes(sources[:, 0, 0], 1, 2)
    targets = lower.shape[1]
    coded_rows = SIDES * block_rows + PAD
    copies_shape = pltpu.VMEM((y_size, SIDES, block_rows, LANES), jnp.bfloat16)

    table_rows = -(-sources.shape[0] * sources.shape[1] // PAD) * PAD
    sent_rows = (2 * levels - 1) * block_rows + table_rows
    first, mine, sent, early = pl.pallas_call(
        first_kernel,
        out_shape=(
            pltpu.VMEM((block_rows, width), jnp.float32),
            pltpu.VMEM((levels, block_rows, LANES), jnp.bfloat16),
            pltpu.VMEM((sent_rows, LANES), jnp.float32),
            pltpu.VMEM((1,) + lower.shape[1:], lower.dtype),
        ),
        in_specs=[ANY, ANY, ANY, VMEM],
        out_specs=(VMEM,) * 4,
        scratch_shapes=[
            pltpu.VMEM(rhs.shape, rhs.dtype),
            pltpu.VMEM(dinv.shape, dinv.dtype),
            pltpu.SemaphoreType.DMA((3,)),
        ],
        compiler_params=PARAMS,
        name="first",
    )(in_hbm(rhs), in_hbm(dinv), in_hbm(lower), in_hbm(sources))
    swapped = in_vmem(lax.all_gather(sent, "core", axis=0, tiled=False))
    mine = in_vmem(mine)
    copies, table = pl.pallas_call(
        spread_kernel,
        out_shape=(copies_shape, pltpu.VMEM((SIDES, table_rows, LANES), jnp.int32)),
        in_specs=[VMEM] * 3,
        out_specs=(VMEM, VMEM),
        compiler_params=PARAMS,
        name="spread",
    )(mine, swapped, sources)
    copies, lower_sent = lax.optimization_barrier((copies, lower))
    other_lower = lax.ppermute(lower_sent, "core", [(0, 1), (1, 0)])

    gathered, solutions = [], []
    for level in range(1, levels):
        blocks = lax.all_to_all(copies, "y", split_axis=0, concat_axis=0, tiled=True)
        gathered.append(in_vmem(blocks.reshape(y_size * SIDES, block_rows, LANES)))
        pairs = tuple(pair_of[earlier, level] for earlier in range(level))
        own = early if level == 1 else lower
        coded = pl.pallas_call(
            functools.partial(terms_kernel, pairs, (za_size, zb_size)),
            out_shape=pltpu.VMEM((targets, coded_rows, LANES), jnp.int16),
            in_specs=[SMEM] + [VMEM] * (SIDES + len(gathered)),
            out_specs=VMEM,
            scratch_shapes=[
                pltpu.VMEM((level, y_size * SIDES + 1, block_rows, LANES), jnp.bfloat16)
            ],
            compiler_params=PARAMS,
            name="local_terms",
        )(table, in_vmem(own), in_vmem(other_lower), *gathered)
        coded = coded.reshape(x_size * zb_size, za_size, coded_rows, LANES)
        arrived = lax.all_to_all(coded, ("x", "zb"), split_axis=0, concat_axis=0, tiled=True)
        coded = pl.pallas_call(
            middle_kernel,
            out_shape=pltpu.VMEM((za_size, coded_rows, LANES), jnp.int16),
            in_specs=[VMEM],
            out_specs=VMEM,
            compiler_params=PARAMS,
            name="sum_near",
        )(in_vmem(arrived))
        arrived = lax.all_to_all(coded, "za", split_axis=0, concat_axis=0, tiled=True)
        operands = [mine, swapped] + [in_vmem(array) for array in (dinv, arrived)]
        if level + 1 < levels:
            solution, copies = pl.pallas_call(
                functools.partial(solve_kernel, level),
                out_shape=(pltpu.VMEM((SIDES, block_rows, LANES), jnp.float32), copies_shape),
                in_specs=[VMEM] * 4,
                out_specs=(VMEM, VMEM),
                compiler_params=PARAMS,
                name="solve",
            )(*operands)
            solutions.append(solution)
        else:
            parts = pl.pallas_call(
                last_kernel,
                out_shape=(pltpu.VMEM((levels - 1, block_rows, LANES), jnp.float32),) * SIDES,
                in_specs=[VMEM] * (4 + len(solutions)),
                out_specs=(VMEM,) * SIDES,
                compiler_params=PARAMS,
                name="solve_last",
            )(*operands, *map(in_vmem, solutions))
    halves = lax.all_gather(parts[1], "core", axis=0, tiled=False)
    joined = pl.pallas_call(
        join_kernel,
        out_shape=jax.ShapeDtypeStruct((levels, block_rows, width), jnp.float32),
        in_specs=[VMEM] * 3,
        out_specs=ANY,
        scratch_shapes=[pltpu.SemaphoreType.DMA((1 + SIDES,))],
        compiler_params=PARAMS,
        name="join",
    )(in_vmem(first), in_vmem(parts[0]), in_vmem(halves))
    return joined[:, None, None]


def solution(mesh):
    split = Mesh(mesh.devices.reshape(8, 2, 4, 4, 2), ("y", "core", "x", "za", "zb"))
    row, col = ("y", "core"), ("x", "za", "zb")
    in_specs = (
        P(None, row, col, None, None),
        P(None, row, col, None, None),
        P(None, row, col, None, None, None),
        P(None, row, col, None, None),
    )
    out_specs = P(None, row, col, None, None)
    return jax.shard_map(
        on_device, mesh=split, in_specs=in_specs, out_specs=out_specs, check_vma=False
    )
```

```python
import functools

import jax
import jax.numpy as jnp
from jax import lax
from jax.experimental import pallas as pl
from jax.experimental.pallas import tpu as pltpu
from jax.sharding import Mesh, PartitionSpec as P

LANES = 128
PAD = 8
SIDES = 2
KERNEL_VMEM = 12 << 20
VMEM = pl.BlockSpec(memory_space=pltpu.VMEM)
SMEM = pl.BlockSpec(memory_space=pltpu.SMEM)
ANY = pl.BlockSpec(memory_space=pl.ANY)
PARAMS = pltpu.CompilerParams(vmem_limit_bytes=KERNEL_VMEM)


MESH_AXES = ("y", "core", "x", "z")
NEAR_Z = 2


def exchange_groups(sizes):
    y_size, cores, x_size, z_size = sizes
    far = z_size // NEAR_Z
    near_first = [[(x, f * NEAR_Z + n) for x in range(x_size) for n in range(NEAR_Z)] for f in range(far)]
    far_last = [[(x, f * NEAR_Z + n) for f in range(far)] for x in range(x_size) for n in range(NEAR_Z)]
    z_first = [[(x, z) for z in range(z_size)] for x in range(x_size)]
    x_last = [[(x, z) for x in range(x_size)] for z in range(z_size)]
    stages = []
    for plans in ((near_first, z_first), (far_last, x_last)):
        stages.append(
            [
                [((y * cores + core) * x_size + x) * z_size + z for x, z in group]
                for y in range(y_size)
                for core in range(cores)
                for group in plans[core]
            ]
        )
    return stages


def in_vmem(array):
    return pltpu.with_memory_space_constraint(array, pltpu.VMEM)


def in_hbm(array):
    return pltpu.with_memory_space_constraint(array, pltpu.HBM)


def encode(parts, out_ref, index):
    powers = []
    for side, part in enumerate(parts):
        rows = part.shape[0]
        largest = jnp.max(jnp.abs(part), axis=0, keepdims=True)
        power = jnp.ceil(jnp.log2(jnp.maximum(largest * 1.001, 1e-30)))
        coded = jnp.round(part * jnp.exp2(15.0 - power)).astype(jnp.int32)
        out_ref[index, side * rows : (side + 1) * rows, :] = coded.astype(jnp.int16)
        powers.append(jnp.broadcast_to(power, (PAD // len(parts), LANES)))
    powers = jnp.concatenate(powers, axis=0).astype(jnp.int32)
    out_ref[index, len(parts) * rows : len(parts) * rows + PAD, :] = powers.astype(jnp.int16)


def decode(block):
    rows = (block.shape[0] - PAD) // SIDES
    powers = block[SIDES * rows :, :].astype(jnp.int32).astype(jnp.float32)
    scales = jnp.exp2(powers - 15.0)
    parts = []
    for side in range(SIDES):
        coded = block[side * rows : (side + 1) * rows, :].astype(jnp.int32).astype(jnp.float32)
        first = side * (PAD // SIDES)
        parts.append(coded * scales[first : first + 1, :])
    return parts


def add_peers(peers, load):
    total = None
    for peer in range(peers):
        parts = decode(load(peer))
        total = parts if total is None else [a + b for a, b in zip(total, parts)]
    return total


def first_kernel(rhs_hbm, dinv_hbm, lower_hbm, sources_ref, *refs):
    solution_ref, mine_ref, sent_ref, factors_ref, rhs_ref, dinv_ref, sems = refs
    copies = [
        pltpu.make_async_copy(rhs_hbm, rhs_ref, sems.at[0]),
        pltpu.make_async_copy(dinv_hbm, dinv_ref, sems.at[1]),
    ]
    early = pltpu.make_async_copy(
        lower_hbm.at[pl.ds(0, factors_ref.shape[0])], factors_ref, sems.at[2]
    )
    for copy in (*copies, early):
        copy.start()
    levels, block_rows, _ = rhs_ref.shape
    base = levels * block_rows
    sent_ref[base:, :] = jnp.zeros((sent_ref.shape[0] - base, LANES), jnp.float32)
    tables = base + (levels - 1) * block_rows
    pairs, per, targets = sources_ref.shape
    for pair in range(pairs):
        rows = slice(tables + pair * per, tables + (pair + 1) * per)
        sent_ref[rows, 0:targets] = sources_ref[pair].astype(jnp.float32)
    for copy in copies:
        copy.wait()
    solution = jnp.dot(
        dinv_ref[0],
        rhs_ref[0].astype(jnp.float32),
        precision=lax.Precision.HIGHEST,
        preferred_element_type=jnp.float32,
    )
    solution_ref[...] = solution
    left_is_mine = lax.axis_index("core") == 0
    for level in range(levels):
        block = rhs_ref[level].astype(jnp.float32) if level else solution
        left, right = block[:, :LANES], block[:, LANES:]
        mine_ref[level] = jnp.where(left_is_mine, left, right).astype(jnp.bfloat16)
        rows = slice(level * block_rows, (level + 1) * block_rows)
        sent_ref[rows, :] = jnp.where(left_is_mine, right, left)
        if level:
            rows = slice(base + (level - 1) * block_rows, base + level * block_rows)
            sent_ref[rows, 0:block_rows] = dinv_ref[level]
    early.wait()


def spread_kernel(mine_ref, swapped_ref, sources_ref, copies_ref, table_ref):
    core = lax.axis_index("core")
    block_rows = mine_ref.shape[1]
    other = swapped_ref.at[1 - core]
    blocks = mine_ref[0], other[0:block_rows, :].astype(jnp.bfloat16)
    for side, block in enumerate(blocks):
        for peer in range(copies_ref.shape[0]):
            copies_ref[peer, side] = block
    none = SIDES * copies_ref.shape[0]

    def places(sources):
        return jnp.where(sources >= 0, jnp.bitwise_xor(sources, core), none)

    pairs, per, targets = sources_ref.shape
    rows = table_ref.shape[1]
    table_ref[0] = jnp.zeros(table_ref.shape[1:], jnp.int32)
    for pair in range(pairs):
        table_ref[0, pair * per : (pair + 1) * per, 0:targets] = places(sources_ref[pair])
    table_ref[1] = places(other[other.shape[0] - rows :, :].astype(jnp.int32))


def terms_kernel(pairs, x_size, table_ref, *refs):
    lowers, gathered, (out_ref, blocks_ref) = refs[:SIDES], refs[SIDES:-2], refs[-2:]
    _, targets, block_rows, depth = lowers[0].shape
    per = depth // block_rows
    z_size = targets // x_size
    far = z_size // NEAR_Z
    near_first = lax.axis_index("core") == 0
    none = blocks_ref.shape[1] - 1
    for place, block in enumerate(gathered):
        blocks_ref[place, 0:none] = block[...]
        blocks_ref[place, none] = jnp.zeros(blocks_ref.shape[2:], blocks_ref.dtype)

    def one(target, carry):
        z = lax.rem(target, z_size)
        near_slot = target - z + lax.rem(z, NEAR_Z) * far + lax.div(z, NEAR_Z)
        slot = jnp.where(near_first, near_slot, z * x_size + lax.div(target, z_size))
        parts = []
        for side in range(SIDES):
            factors, picked = [], []
            for place, pair in enumerate(pairs):
                factors.append(lowers[side][pair, target])
                for entry in range(per):
                    picked.append(blocks_ref[place, table_ref[side, pair * per + entry, target]])
            parts.append(
                jnp.dot(
                    jnp.concatenate(factors, axis=1),
                    jnp.concatenate(picked, axis=0),
                    preferred_element_type=jnp.float32,
                )
            )
        encode(parts, out_ref, slot)
        return carry

    lax.fori_loop(0, targets, one, 0, unroll=True)


def middle_kernel(arrived_ref, out_ref):
    peers, targets = arrived_ref.shape[:2]
    for target in range(targets):
        encode(add_peers(peers, lambda peer: arrived_ref[peer, target]), out_ref, target)


def solve_parts(level, mine_ref, swapped_ref, dinv_ref, arrived_ref):
    levels, block_rows, _ = mine_ref.shape
    other = swapped_ref.at[1 - lax.axis_index("core")]
    base = (levels + level - 1) * block_rows
    blocks = mine_ref[level].astype(jnp.float32), other[level * block_rows : (level + 1) * block_rows, :]
    factors = dinv_ref[level], other[base : base + block_rows, 0:block_rows]
    total = add_peers(arrived_ref.shape[0], lambda peer: arrived_ref[peer])
    return [
        jnp.dot(
            factor,
            block - part,
            precision=lax.Precision.HIGHEST,
            preferred_element_type=jnp.float32,
        )
        for factor, block, part in zip(factors, blocks, total)
    ]


def solve_kernel(level, mine_ref, swapped_ref, dinv_ref, arrived_ref, solution_ref, copies_ref):
    parts = solve_parts(level, mine_ref, swapped_ref, dinv_ref, arrived_ref)
    for side, part in enumerate(parts):
        solution_ref[side] = part
        for peer in range(copies_ref.shape[0]):
            copies_ref[peer, side] = part.astype(jnp.bfloat16)


def last_kernel(mine_ref, swapped_ref, dinv_ref, arrived_ref, *refs):
    earlier, outs = refs[:-SIDES], refs[-SIDES:]
    for place, ref in enumerate(earlier):
        for side, out_ref in enumerate(outs):
            out_ref[place] = ref[side]
    level = len(earlier) + 1
    parts = solve_parts(level, mine_ref, swapped_ref, dinv_ref, arrived_ref)
    for part, out_ref in zip(parts, outs):
        out_ref[level - 1] = part


def join_kernel(first_ref, mine_ref, swapped_ref, out_ref, sems):
    core = lax.axis_index("core")
    later = pl.ds(1, mine_ref.shape[0])
    copies = [pltpu.make_async_copy(first_ref, out_ref.at[0], sems.at[0])]
    for index, (half, ref) in enumerate(((core, mine_ref), (1 - core, swapped_ref.at[1 - core]))):
        columns = pl.ds(pl.multiple_of(half * LANES, LANES), LANES)
        copies.append(pltpu.make_async_copy(ref, out_ref.at[later, :, columns], sems.at[1 + index]))
    for copy in copies:
        copy.start()
    for copy in copies:
        copy.wait()


def on_device(rhs, dinv, lower, sources):
    levels, _, _, block_rows, width = rhs.shape
    sizes = tuple(lax.axis_size(name) for name in MESH_AXES)
    y_size, _, x_size, _ = sizes
    first_groups, second_groups = exchange_groups(sizes)
    first_peers, second_peers = len(first_groups[0]), len(second_groups[0])

    def exchange(array, groups):
        return lax.all_to_all(
            array, MESH_AXES, split_axis=0, concat_axis=0, axis_index_groups=groups, tiled=True
        )

    pair_of = {}
    for section in range(levels):
        for target in range(section + 1, levels):
            pair_of[section, target] = len(pair_of)
    rhs, dinv, lower = rhs[:, 0, 0], dinv[:, 0, 0], lower[:, 0, 0]
    sources = jnp.swapaxes(sources[:, 0, 0], 1, 2)
    targets = lower.shape[1]
    coded_rows = SIDES * block_rows + PAD
    copies_shape = pltpu.VMEM((y_size, SIDES, block_rows, LANES), jnp.bfloat16)

    table_rows = -(-sources.shape[0] * sources.shape[1] // PAD) * PAD
    sent_rows = (2 * levels - 1) * block_rows + table_rows
    first, mine, sent, early = pl.pallas_call(
        first_kernel,
        out_shape=(
            pltpu.VMEM((block_rows, width), jnp.float32),
            pltpu.VMEM((levels, block_rows, LANES), jnp.bfloat16),
            pltpu.VMEM((sent_rows, LANES), jnp.float32),
            pltpu.VMEM((1,) + lower.shape[1:], lower.dtype),
        ),
        in_specs=[ANY, ANY, ANY, VMEM],
        out_specs=(VMEM,) * 4,
        scratch_shapes=[
            pltpu.VMEM(rhs.shape, rhs.dtype),
            pltpu.VMEM(dinv.shape, dinv.dtype),
            pltpu.SemaphoreType.DMA((3,)),
        ],
        compiler_params=PARAMS,
        name="first",
    )(in_hbm(rhs), in_hbm(dinv), in_hbm(lower), in_hbm(sources))
    swapped = in_vmem(lax.all_gather(sent, "core", axis=0, tiled=False))
    mine = in_vmem(mine)
    copies, table = pl.pallas_call(
        spread_kernel,
        out_shape=(copies_shape, pltpu.VMEM((SIDES, table_rows, LANES), jnp.int32)),
        in_specs=[VMEM] * 3,
        out_specs=(VMEM, VMEM),
        compiler_params=PARAMS,
        name="spread",
    )(mine, swapped, sources)
    copies, lower_sent = lax.optimization_barrier((copies, lower))
    other_lower = lax.ppermute(lower_sent, "core", [(0, 1), (1, 0)])

    gathered, solutions = [], []
    for level in range(1, levels):
        blocks = lax.all_to_all(copies, "y", split_axis=0, concat_axis=0, tiled=True)
        gathered.append(in_vmem(blocks.reshape(y_size * SIDES, block_rows, LANES)))
        pairs = tuple(pair_of[earlier, level] for earlier in range(level))
        own = early if level == 1 else lower
        coded = pl.pallas_call(
            functools.partial(terms_kernel, pairs, x_size),
            out_shape=pltpu.VMEM((targets, coded_rows, LANES), jnp.int16),
            in_specs=[SMEM] + [VMEM] * (SIDES + len(gathered)),
            out_specs=VMEM,
            scratch_shapes=[
                pltpu.VMEM((level, y_size * SIDES + 1, block_rows, LANES), jnp.bfloat16)
            ],
            compiler_params=PARAMS,
            name="local_terms",
        )(table, in_vmem(own), in_vmem(other_lower), *gathered)
        coded = coded.reshape(first_peers, second_peers, coded_rows, LANES)
        arrived = exchange(coded, first_groups)
        coded = pl.pallas_call(
            middle_kernel,
            out_shape=pltpu.VMEM((second_peers, coded_rows, LANES), jnp.int16),
            in_specs=[VMEM],
            out_specs=VMEM,
            compiler_params=PARAMS,
            name="sum_first",
        )(in_vmem(arrived))
        arrived = exchange(coded, second_groups)
        operands = [mine, swapped] + [in_vmem(array) for array in (dinv, arrived)]
        if level + 1 < levels:
            solution, copies = pl.pallas_call(
                functools.partial(solve_kernel, level),
                out_shape=(pltpu.VMEM((SIDES, block_rows, LANES), jnp.float32), copies_shape),
                in_specs=[VMEM] * 4,
                out_specs=(VMEM, VMEM),
                compiler_params=PARAMS,
                name="solve",
            )(*operands)
            solutions.append(solution)
        else:
            parts = pl.pallas_call(
                last_kernel,
                out_shape=(pltpu.VMEM((levels - 1, block_rows, LANES), jnp.float32),) * SIDES,
                in_specs=[VMEM] * (4 + len(solutions)),
                out_specs=(VMEM,) * SIDES,
                compiler_params=PARAMS,
                name="solve_last",
            )(*operands, *map(in_vmem, solutions))
    halves = lax.all_gather(parts[1], "core", axis=0, tiled=False)
    joined = pl.pallas_call(
        join_kernel,
        out_shape=jax.ShapeDtypeStruct((levels, block_rows, width), jnp.float32),
        in_specs=[VMEM] * 3,
        out_specs=ANY,
        scratch_shapes=[pltpu.SemaphoreType.DMA((1 + SIDES,))],
        compiler_params=PARAMS,
        name="join",
    )(in_vmem(first), in_vmem(parts[0]), in_vmem(halves))
    return joined[:, None, None]


def solution(mesh):
    split = Mesh(mesh.devices.reshape(8, 2, 4, 8), MESH_AXES)
    row, col = MESH_AXES[:2], MESH_AXES[2:]
    in_specs = (
        P(None, row, col, None, None),
        P(None, row, col, None, None),
        P(None, row, col, None, None, None),
        P(None, row, col, None, None),
    )
    out_specs = P(None, row, col, None, None)
    return jax.shard_map(
        on_device, mesh=split, in_specs=in_specs, out_specs=out_specs, check_vma=False
    )
```

```python
import functools

import jax
import jax.numpy as jnp
from jax import lax
from jax.experimental import pallas as pl
from jax.experimental.pallas import tpu as pltpu
from jax.sharding import Mesh, PartitionSpec as P

LANES = 128
PAD = 8
SIDES = 2
KERNEL_VMEM = 12 << 20
VMEM = pl.BlockSpec(memory_space=pltpu.VMEM)
SMEM = pl.BlockSpec(memory_space=pltpu.SMEM)
ANY = pl.BlockSpec(memory_space=pl.ANY)
PARAMS = pltpu.CompilerParams(vmem_limit_bytes=KERNEL_VMEM)


MESH_AXES = ("y", "core", "x", "z")
NEAR_Z = 2


def exchange_groups(sizes):
    y_size, cores, x_size, z_size = sizes
    far = z_size // NEAR_Z
    first, second = [], []
    for y in range(y_size):
        for core in range(cores):

            def device(x, f, n):
                z = (f * NEAR_Z + n + core) % z_size
                return ((y * cores + core) * x_size + x) * z_size + z

            for f in range(far):
                first.append([device(x, f, n) for x in range(x_size) for n in range(NEAR_Z)])
            for x in range(x_size):
                for n in range(NEAR_Z):
                    second.append([device(x, f, n) for f in range(far)])
    return first, second


def in_vmem(array):
    return pltpu.with_memory_space_constraint(array, pltpu.VMEM)


def in_hbm(array):
    return pltpu.with_memory_space_constraint(array, pltpu.HBM)


def encode(parts, out_ref, index):
    powers = []
    for side, part in enumerate(parts):
        rows = part.shape[0]
        largest = jnp.max(jnp.abs(part), axis=0, keepdims=True)
        power = jnp.ceil(jnp.log2(jnp.maximum(largest * 1.001, 1e-30)))
        coded = jnp.round(part * jnp.exp2(15.0 - power)).astype(jnp.int32)
        out_ref[index, side * rows : (side + 1) * rows, :] = coded.astype(jnp.int16)
        powers.append(jnp.broadcast_to(power, (PAD // len(parts), LANES)))
    powers = jnp.concatenate(powers, axis=0).astype(jnp.int32)
    out_ref[index, len(parts) * rows : len(parts) * rows + PAD, :] = powers.astype(jnp.int16)


def decode(block):
    rows = (block.shape[0] - PAD) // SIDES
    powers = block[SIDES * rows :, :].astype(jnp.int32).astype(jnp.float32)
    scales = jnp.exp2(powers - 15.0)
    parts = []
    for side in range(SIDES):
        coded = block[side * rows : (side + 1) * rows, :].astype(jnp.int32).astype(jnp.float32)
        first = side * (PAD // SIDES)
        parts.append(coded * scales[first : first + 1, :])
    return parts


def add_peers(peers, load):
    total = None
    for peer in range(peers):
        parts = decode(load(peer))
        total = parts if total is None else [a + b for a, b in zip(total, parts)]
    return total


def first_kernel(rhs_hbm, dinv_hbm, lower_hbm, sources_ref, *refs):
    solution_ref, mine_ref, sent_ref, factors_ref, rhs_ref, dinv_ref, sems = refs
    copies = [
        pltpu.make_async_copy(rhs_hbm, rhs_ref, sems.at[0]),
        pltpu.make_async_copy(dinv_hbm, dinv_ref, sems.at[1]),
    ]
    early = pltpu.make_async_copy(
        lower_hbm.at[pl.ds(0, factors_ref.shape[0])], factors_ref, sems.at[2]
    )
    for copy in (*copies, early):
        copy.start()
    levels, block_rows, _ = rhs_ref.shape
    base = levels * block_rows
    sent_ref[base:, :] = jnp.zeros((sent_ref.shape[0] - base, LANES), jnp.float32)
    tables = base + (levels - 1) * block_rows
    pairs, per, targets = sources_ref.shape
    for pair in range(pairs):
        rows = slice(tables + pair * per, tables + (pair + 1) * per)
        sent_ref[rows, 0:targets] = sources_ref[pair].astype(jnp.float32)
    for copy in copies:
        copy.wait()
    solution = jnp.dot(
        dinv_ref[0],
        rhs_ref[0].astype(jnp.float32),
        precision=lax.Precision.HIGHEST,
        preferred_element_type=jnp.float32,
    )
    solution_ref[...] = solution
    left_is_mine = lax.axis_index("core") == 0
    for level in range(levels):
        block = rhs_ref[level].astype(jnp.float32) if level else solution
        left, right = block[:, :LANES], block[:, LANES:]
        mine_ref[level] = jnp.where(left_is_mine, left, right).astype(jnp.bfloat16)
        rows = slice(level * block_rows, (level + 1) * block_rows)
        sent_ref[rows, :] = jnp.where(left_is_mine, right, left)
        if level:
            rows = slice(base + (level - 1) * block_rows, base + level * block_rows)
            sent_ref[rows, 0:block_rows] = dinv_ref[level]
    early.wait()


def spread_kernel(mine_ref, swapped_ref, sources_ref, copies_ref, table_ref):
    core = lax.axis_index("core")
    block_rows = mine_ref.shape[1]
    other = swapped_ref.at[1 - core]
    blocks = mine_ref[0], other[0:block_rows, :].astype(jnp.bfloat16)
    for side, block in enumerate(blocks):
        for peer in range(copies_ref.shape[0]):
            copies_ref[peer, side] = block
    none = SIDES * copies_ref.shape[0]

    def places(sources):
        return jnp.where(sources >= 0, jnp.bitwise_xor(sources, core), none)

    pairs, per, targets = sources_ref.shape
    rows = table_ref.shape[1]
    table_ref[0] = jnp.zeros(table_ref.shape[1:], jnp.int32)
    for pair in range(pairs):
        table_ref[0, pair * per : (pair + 1) * per, 0:targets] = places(sources_ref[pair])
    table_ref[1] = places(other[other.shape[0] - rows :, :].astype(jnp.int32))


def terms_kernel(pairs, x_size, table_ref, *refs):
    lowers, gathered, (out_ref, blocks_ref) = refs[:SIDES], refs[SIDES:-2], refs[-2:]
    _, targets, block_rows, depth = lowers[0].shape
    per = depth // block_rows
    z_size = targets // x_size
    far = z_size // NEAR_Z
    core = lax.axis_index("core")
    none = blocks_ref.shape[1] - 1
    for place, block in enumerate(gathered):
        blocks_ref[place, 0:none] = block[...]
        blocks_ref[place, none] = jnp.zeros(blocks_ref.shape[2:], blocks_ref.dtype)

    def one(target, carry):
        x = lax.div(target, z_size)
        z = lax.rem(target + z_size - core, z_size)
        slot = x * z_size + lax.rem(z, NEAR_Z) * far + lax.div(z, NEAR_Z)
        parts = []
        for side in range(SIDES):
            factors, picked = [], []
            for place, pair in enumerate(pairs):
                factors.append(lowers[side][pair, target])
                for entry in range(per):
                    picked.append(blocks_ref[place, table_ref[side, pair * per + entry, target]])
            parts.append(
                jnp.dot(
                    jnp.concatenate(factors, axis=1),
                    jnp.concatenate(picked, axis=0),
                    preferred_element_type=jnp.float32,
                )
            )
        encode(parts, out_ref, slot)
        return carry

    lax.fori_loop(0, targets, one, 0, unroll=True)


def middle_kernel(arrived_ref, out_ref):
    peers, targets = arrived_ref.shape[:2]
    for target in range(targets):
        encode(add_peers(peers, lambda peer: arrived_ref[peer, target]), out_ref, target)


def solve_parts(level, mine_ref, swapped_ref, dinv_ref, arrived_ref):
    levels, block_rows, _ = mine_ref.shape
    other = swapped_ref.at[1 - lax.axis_index("core")]
    base = (levels + level - 1) * block_rows
    blocks = mine_ref[level].astype(jnp.float32), other[level * block_rows : (level + 1) * block_rows, :]
    factors = dinv_ref[level], other[base : base + block_rows, 0:block_rows]
    total = add_peers(arrived_ref.shape[0], lambda peer: arrived_ref[peer])
    return [
        jnp.dot(
            factor,
            block - part,
            precision=lax.Precision.HIGHEST,
            preferred_element_type=jnp.float32,
        )
        for factor, block, part in zip(factors, blocks, total)
    ]


def solve_kernel(level, mine_ref, swapped_ref, dinv_ref, arrived_ref, solution_ref, copies_ref):
    parts = solve_parts(level, mine_ref, swapped_ref, dinv_ref, arrived_ref)
    for side, part in enumerate(parts):
        solution_ref[side] = part
        for peer in range(copies_ref.shape[0]):
            copies_ref[peer, side] = part.astype(jnp.bfloat16)


def last_kernel(mine_ref, swapped_ref, dinv_ref, arrived_ref, *refs):
    earlier, outs = refs[:-SIDES], refs[-SIDES:]
    for place, ref in enumerate(earlier):
        for side, out_ref in enumerate(outs):
            out_ref[place] = ref[side]
    level = len(earlier) + 1
    parts = solve_parts(level, mine_ref, swapped_ref, dinv_ref, arrived_ref)
    for part, out_ref in zip(parts, outs):
        out_ref[level - 1] = part


def join_kernel(first_ref, mine_ref, swapped_ref, out_ref, sems):
    core = lax.axis_index("core")
    later = pl.ds(1, mine_ref.shape[0])
    copies = [pltpu.make_async_copy(first_ref, out_ref.at[0], sems.at[0])]
    for index, (half, ref) in enumerate(((core, mine_ref), (1 - core, swapped_ref.at[1 - core]))):
        columns = pl.ds(pl.multiple_of(half * LANES, LANES), LANES)
        copies.append(pltpu.make_async_copy(ref, out_ref.at[later, :, columns], sems.at[1 + index]))
    for copy in copies:
        copy.start()
    for copy in copies:
        copy.wait()


def on_device(rhs, dinv, lower, sources):
    levels, _, _, block_rows, width = rhs.shape
    sizes = tuple(lax.axis_size(name) for name in MESH_AXES)
    y_size, _, x_size, _ = sizes
    first_groups, second_groups = exchange_groups(sizes)
    first_peers, second_peers = len(first_groups[0]), len(second_groups[0])

    def exchange(array, groups):
        return lax.all_to_all(
            array, MESH_AXES, split_axis=0, concat_axis=0, axis_index_groups=groups, tiled=True
        )

    pair_of = {}
    for section in range(levels):
        for target in range(section + 1, levels):
            pair_of[section, target] = len(pair_of)
    rhs, dinv, lower = rhs[:, 0, 0], dinv[:, 0, 0], lower[:, 0, 0]
    sources = jnp.swapaxes(sources[:, 0, 0], 1, 2)
    targets = lower.shape[1]
    coded_rows = SIDES * block_rows + PAD
    copies_shape = pltpu.VMEM((y_size, SIDES, block_rows, LANES), jnp.bfloat16)

    table_rows = -(-sources.shape[0] * sources.shape[1] // PAD) * PAD
    sent_rows = (2 * levels - 1) * block_rows + table_rows
    first, mine, sent, early = pl.pallas_call(
        first_kernel,
        out_shape=(
            pltpu.VMEM((block_rows, width), jnp.float32),
            pltpu.VMEM((levels, block_rows, LANES), jnp.bfloat16),
            pltpu.VMEM((sent_rows, LANES), jnp.float32),
            pltpu.VMEM((1,) + lower.shape[1:], lower.dtype),
        ),
        in_specs=[ANY, ANY, ANY, VMEM],
        out_specs=(VMEM,) * 4,
        scratch_shapes=[
            pltpu.VMEM(rhs.shape, rhs.dtype),
            pltpu.VMEM(dinv.shape, dinv.dtype),
            pltpu.SemaphoreType.DMA((3,)),
        ],
        compiler_params=PARAMS,
        name="first",
    )(in_hbm(rhs), in_hbm(dinv), in_hbm(lower), in_hbm(sources))
    swapped = in_vmem(lax.all_gather(sent, "core", axis=0, tiled=False))
    mine = in_vmem(mine)
    copies, table = pl.pallas_call(
        spread_kernel,
        out_shape=(copies_shape, pltpu.VMEM((SIDES, table_rows, LANES), jnp.int32)),
        in_specs=[VMEM] * 3,
        out_specs=(VMEM, VMEM),
        compiler_params=PARAMS,
        name="spread",
    )(mine, swapped, sources)
    copies, lower_sent = lax.optimization_barrier((copies, lower))
    other_lower = lax.ppermute(lower_sent, "core", [(0, 1), (1, 0)])

    gathered, solutions = [], []
    for level in range(1, levels):
        blocks = lax.all_to_all(copies, "y", split_axis=0, concat_axis=0, tiled=True)
        gathered.append(in_vmem(blocks.reshape(y_size * SIDES, block_rows, LANES)))
        pairs = tuple(pair_of[earlier, level] for earlier in range(level))
        own = early if level == 1 else lower
        coded = pl.pallas_call(
            functools.partial(terms_kernel, pairs, x_size),
            out_shape=pltpu.VMEM((targets, coded_rows, LANES), jnp.int16),
            in_specs=[SMEM] + [VMEM] * (SIDES + len(gathered)),
            out_specs=VMEM,
            scratch_shapes=[
                pltpu.VMEM((level, y_size * SIDES + 1, block_rows, LANES), jnp.bfloat16)
            ],
            compiler_params=PARAMS,
            name="local_terms",
        )(table, in_vmem(own), in_vmem(other_lower), *gathered)
        coded = coded.reshape(first_peers, second_peers, coded_rows, LANES)
        arrived = exchange(coded, first_groups)
        coded = pl.pallas_call(
            middle_kernel,
            out_shape=pltpu.VMEM((second_peers, coded_rows, LANES), jnp.int16),
            in_specs=[VMEM],
            out_specs=VMEM,
            compiler_params=PARAMS,
            name="sum_first",
        )(in_vmem(arrived))
        arrived = exchange(coded, second_groups)
        operands = [mine, swapped] + [in_vmem(array) for array in (dinv, arrived)]
        if level + 1 < levels:
            solution, copies = pl.pallas_call(
                functools.partial(solve_kernel, level),
                out_shape=(pltpu.VMEM((SIDES, block_rows, LANES), jnp.float32), copies_shape),
                in_specs=[VMEM] * 4,
                out_specs=(VMEM, VMEM),
                compiler_params=PARAMS,
                name="solve",
            )(*operands)
            solutions.append(solution)
        else:
            parts = pl.pallas_call(
                last_kernel,
                out_shape=(pltpu.VMEM((levels - 1, block_rows, LANES), jnp.float32),) * SIDES,
                in_specs=[VMEM] * (4 + len(solutions)),
                out_specs=(VMEM,) * SIDES,
                compiler_params=PARAMS,
                name="solve_last",
            )(*operands, *map(in_vmem, solutions))
    halves = lax.all_gather(parts[1], "core", axis=0, tiled=False)
    joined = pl.pallas_call(
        join_kernel,
        out_shape=jax.ShapeDtypeStruct((levels, block_rows, width), jnp.float32),
        in_specs=[VMEM] * 3,
        out_specs=ANY,
        scratch_shapes=[pltpu.SemaphoreType.DMA((1 + SIDES,))],
        compiler_params=PARAMS,
        name="join",
    )(in_vmem(first), in_vmem(parts[0]), in_vmem(halves))
    return joined[:, None, None]


def solution(mesh):
    split = Mesh(mesh.devices.reshape(8, 2, 4, 8), MESH_AXES)
    row, col = MESH_AXES[:2], MESH_AXES[2:]
    in_specs = (
        P(None, row, col, None, None),
        P(None, row, col, None, None),
        P(None, row, col, None, None, None),
        P(None, row, col, None, None),
    )
    out_specs = P(None, row, col, None, None)
    return jax.shard_map(
        on_device, mesh=split, in_specs=in_specs, out_specs=out_specs, check_vma=False
    )
```

```python
import functools

import jax
import jax.numpy as jnp
from jax import lax
from jax.experimental import pallas as pl
from jax.experimental.pallas import tpu as pltpu
from jax.sharding import Mesh, PartitionSpec as P

LANES = 128
PAD = 8
SIDES = 2
KERNEL_VMEM = 12 << 20
VMEM = pl.BlockSpec(memory_space=pltpu.VMEM)
SMEM = pl.BlockSpec(memory_space=pltpu.SMEM)
ANY = pl.BlockSpec(memory_space=pl.ANY)
PARAMS = pltpu.CompilerParams(vmem_limit_bytes=KERNEL_VMEM)


def in_vmem(array):
    return pltpu.with_memory_space_constraint(array, pltpu.VMEM)


def in_hbm(array):
    return pltpu.with_memory_space_constraint(array, pltpu.HBM)


def code(part):
    largest = jnp.max(jnp.abs(part), axis=0, keepdims=True)
    power = jnp.ceil(jnp.log2(jnp.maximum(largest * 1.001, 1e-30)))
    coded = jnp.round(part * jnp.exp2(15.0 - power)).astype(jnp.int32)
    return coded.astype(jnp.int16), power


def encode(parts, out_ref, index):
    powers = []
    for side, part in enumerate(parts):
        rows = part.shape[0]
        coded, power = code(part)
        out_ref[index, side * rows : (side + 1) * rows, :] = coded
        powers.append(jnp.broadcast_to(power, (PAD // len(parts), LANES)))
    powers = jnp.concatenate(powers, axis=0).astype(jnp.int32)
    out_ref[index, len(parts) * rows : len(parts) * rows + PAD, :] = powers.astype(jnp.int16)


def decode(block):
    rows = (block.shape[0] - PAD) // SIDES
    powers = block[SIDES * rows :, :].astype(jnp.int32).astype(jnp.float32)
    scales = jnp.exp2(powers - 15.0)
    parts = []
    for side in range(SIDES):
        coded = block[side * rows : (side + 1) * rows, :].astype(jnp.int32).astype(jnp.float32)
        first = side * (PAD // SIDES)
        parts.append(coded * scales[first : first + 1, :])
    return parts


def add_peers(peers, load):
    total = None
    for peer in range(peers):
        parts = decode(load(peer))
        total = parts if total is None else [a + b for a, b in zip(total, parts)]
    return total


def first_kernel(rhs_hbm, dinv_hbm, lower_hbm, sources_ref, *refs):
    solution_ref, mine_ref, sent_ref, factors_ref, rhs_ref, dinv_ref, sems = refs
    copies = [
        pltpu.make_async_copy(rhs_hbm, rhs_ref, sems.at[0]),
        pltpu.make_async_copy(dinv_hbm, dinv_ref, sems.at[1]),
    ]
    early = pltpu.make_async_copy(
        lower_hbm.at[pl.ds(0, factors_ref.shape[0])], factors_ref, sems.at[2]
    )
    for copy in (*copies, early):
        copy.start()
    levels, block_rows, _ = rhs_ref.shape
    base = levels * block_rows
    sent_ref[base:, :] = jnp.zeros((sent_ref.shape[0] - base, LANES), jnp.float32)
    tables = base + (levels - 1) * block_rows
    pairs, per, targets = sources_ref.shape
    for pair in range(pairs):
        rows = slice(tables + pair * per, tables + (pair + 1) * per)
        sent_ref[rows, 0:targets] = sources_ref[pair].astype(jnp.float32)
    for copy in copies:
        copy.wait()
    solution = jnp.dot(
        dinv_ref[0],
        rhs_ref[0].astype(jnp.float32),
        precision=lax.Precision.HIGHEST,
        preferred_element_type=jnp.float32,
    )
    solution_ref[...] = solution
    left_is_mine = lax.axis_index("core") == 0
    for level in range(levels):
        block = rhs_ref[level].astype(jnp.float32) if level else solution
        left, right = block[:, :LANES], block[:, LANES:]
        mine_ref[level] = jnp.where(left_is_mine, left, right).astype(jnp.bfloat16)
        rows = slice(level * block_rows, (level + 1) * block_rows)
        sent_ref[rows, :] = jnp.where(left_is_mine, right, left)
        if level:
            rows = slice(base + (level - 1) * block_rows, base + level * block_rows)
            sent_ref[rows, 0:block_rows] = dinv_ref[level]
    early.wait()


def spread_kernel(mine_ref, swapped_ref, sources_ref, copies_ref, table_ref):
    core = lax.axis_index("core")
    block_rows = mine_ref.shape[1]
    other = swapped_ref.at[1 - core]
    blocks = mine_ref[0], other[0:block_rows, :].astype(jnp.bfloat16)
    for side, block in enumerate(blocks):
        for peer in range(copies_ref.shape[0]):
            copies_ref[peer, side] = block
    none = SIDES * copies_ref.shape[0]

    def places(sources):
        return jnp.where(sources >= 0, jnp.bitwise_xor(sources, core), none)

    pairs, per, targets = sources_ref.shape
    rows = table_ref.shape[1]
    table_ref[0] = jnp.zeros(table_ref.shape[1:], jnp.int32)
    for pair in range(pairs):
        table_ref[0, pair * per : (pair + 1) * per, 0:targets] = places(sources_ref[pair])
    table_ref[1] = places(other[other.shape[0] - rows :, :].astype(jnp.int32))


def terms_kernel(pairs, z_sizes, table_ref, *refs):
    lowers, gathered, (out_ref, blocks_ref) = refs[:SIDES], refs[SIDES:-2], refs[-2:]
    _, targets, block_rows, depth = lowers[0].shape
    per = depth // block_rows
    za_size, zb_size = z_sizes
    none = blocks_ref.shape[1] - 1
    for place, block in enumerate(gathered):
        blocks_ref[place, 0:none] = block[...]
        blocks_ref[place, none] = jnp.zeros(blocks_ref.shape[2:], blocks_ref.dtype)

    def sums(target):
        for side in range(SIDES):
            factors, picked = [], []
            for place, pair in enumerate(pairs):
                factors.append(lowers[side][pair, target])
                for entry in range(per):
                    picked.append(blocks_ref[place, table_ref[side, pair * per + entry, target]])
            yield jnp.dot(
                jnp.concatenate(factors, axis=1),
                jnp.concatenate(picked, axis=0),
                preferred_element_type=jnp.float32,
            )

    tail = za_size * SIDES * block_rows
    for peer in range(targets // za_size):
        x, zb = divmod(peer, zb_size)
        powers, row = [], 0
        for za in range(za_size):
            for part in sums((x * za_size + za) * zb_size + zb):
                coded, power = code(part)
                out_ref[peer, row : row + block_rows, :] = coded
                powers.append(power)
                row += block_rows
        powers = jnp.concatenate(powers, axis=0).astype(jnp.int32)
        out_ref[peer, tail : tail + za_size * SIDES, :] = powers.astype(jnp.int16)


def middle_kernel(za_size, arrived_ref, out_ref):
    peers = arrived_ref.shape[0]
    places = za_size * SIDES
    block_rows = arrived_ref.shape[1] // places - 1
    scales = []
    for peer in range(peers):
        powers = arrived_ref[peer, places * block_rows :, :].astype(jnp.int32)
        scales.append(jnp.exp2(powers.astype(jnp.float32) - 15.0))
    for za in range(za_size):
        parts = []
        for place in range(za * SIDES, (za + 1) * SIDES):
            total = None
            for peer in range(peers):
                block = arrived_ref[peer, place * block_rows : (place + 1) * block_rows, :]
                part = block.astype(jnp.int32).astype(jnp.float32) * scales[peer][place : place + 1, :]
                total = part if total is None else total + part
            parts.append(total)
        encode(parts, out_ref, za)


def solve_parts(level, mine_ref, swapped_ref, dinv_ref, arrived_ref):
    levels, block_rows, _ = mine_ref.shape
    other = swapped_ref.at[1 - lax.axis_index("core")]
    base = (levels + level - 1) * block_rows
    blocks = mine_ref[level].astype(jnp.float32), other[level * block_rows : (level + 1) * block_rows, :]
    factors = dinv_ref[level], other[base : base + block_rows, 0:block_rows]
    total = add_peers(arrived_ref.shape[0], lambda peer: arrived_ref[peer])
    return [
        jnp.dot(
            factor,
            block - part,
            precision=lax.Precision.HIGHEST,
            preferred_element_type=jnp.float32,
        )
        for factor, block, part in zip(factors, blocks, total)
    ]


def solve_kernel(level, mine_ref, swapped_ref, dinv_ref, arrived_ref, solution_ref, copies_ref):
    parts = solve_parts(level, mine_ref, swapped_ref, dinv_ref, arrived_ref)
    for side, part in enumerate(parts):
        solution_ref[side] = part
        for peer in range(copies_ref.shape[0]):
            copies_ref[peer, side] = part.astype(jnp.bfloat16)


def last_kernel(mine_ref, swapped_ref, dinv_ref, arrived_ref, *refs):
    earlier, outs = refs[:-SIDES], refs[-SIDES:]
    for place, ref in enumerate(earlier):
        for side, out_ref in enumerate(outs):
            out_ref[place] = ref[side]
    level = len(earlier) + 1
    parts = solve_parts(level, mine_ref, swapped_ref, dinv_ref, arrived_ref)
    for part, out_ref in zip(parts, outs):
        out_ref[level - 1] = part


def join_kernel(first_ref, mine_ref, swapped_ref, out_ref, sems):
    core = lax.axis_index("core")
    later = pl.ds(1, mine_ref.shape[0])
    copies = [pltpu.make_async_copy(first_ref, out_ref.at[0], sems.at[0])]
    for index, (half, ref) in enumerate(((core, mine_ref), (1 - core, swapped_ref.at[1 - core]))):
        columns = pl.ds(pl.multiple_of(half * LANES, LANES), LANES)
        copies.append(pltpu.make_async_copy(ref, out_ref.at[later, :, columns], sems.at[1 + index]))
    for copy in copies:
        copy.start()
    for copy in copies:
        copy.wait()


def on_device(rhs, dinv, lower, sources):
    levels, _, _, block_rows, width = rhs.shape
    y_size, x_size, za_size, zb_size = (lax.axis_size(name) for name in ("y", "x", "za", "zb"))
    pair_of = {}
    for section in range(levels):
        for target in range(section + 1, levels):
            pair_of[section, target] = len(pair_of)
    rhs, dinv, lower = rhs[:, 0, 0], dinv[:, 0, 0], lower[:, 0, 0]
    sources = jnp.swapaxes(sources[:, 0, 0], 1, 2)
    targets = lower.shape[1]
    coded_rows = SIDES * block_rows + PAD
    near_rows = za_size * SIDES * (block_rows + 1)
    copies_shape = pltpu.VMEM((y_size, SIDES, block_rows, LANES), jnp.bfloat16)

    table_rows = -(-sources.shape[0] * sources.shape[1] // PAD) * PAD
    sent_rows = (2 * levels - 1) * block_rows + table_rows
    first, mine, sent, early = pl.pallas_call(
        first_kernel,
        out_shape=(
            pltpu.VMEM((block_rows, width), jnp.float32),
            pltpu.VMEM((levels, block_rows, LANES), jnp.bfloat16),
            pltpu.VMEM((sent_rows, LANES), jnp.float32),
            pltpu.VMEM((1,) + lower.shape[1:], lower.dtype),
        ),
        in_specs=[ANY, ANY, ANY, VMEM],
        out_specs=(VMEM,) * 4,
        scratch_shapes=[
            pltpu.VMEM(rhs.shape, rhs.dtype),
            pltpu.VMEM(dinv.shape, dinv.dtype),
            pltpu.SemaphoreType.DMA((3,)),
        ],
        compiler_params=PARAMS,
        name="first",
    )(in_hbm(rhs), in_hbm(dinv), in_hbm(lower), in_hbm(sources))
    swapped = in_vmem(lax.all_gather(sent, "core", axis=0, tiled=False))
    mine = in_vmem(mine)
    copies, table = pl.pallas_call(
        spread_kernel,
        out_shape=(copies_shape, pltpu.VMEM((SIDES, table_rows, LANES), jnp.int32)),
        in_specs=[VMEM] * 3,
        out_specs=(VMEM, VMEM),
        compiler_params=PARAMS,
        name="spread",
    )(mine, swapped, sources)
    copies, lower_sent = lax.optimization_barrier((copies, lower))
    other_lower = lax.ppermute(lower_sent, "core", [(0, 1), (1, 0)])

    gathered, solutions = [], []
    for level in range(1, levels):
        blocks = lax.all_to_all(copies, "y", split_axis=0, concat_axis=0, tiled=True)
        gathered.append(in_vmem(blocks.reshape(y_size * SIDES, block_rows, LANES)))
        pairs = tuple(pair_of[earlier, level] for earlier in range(level))
        own = early if level == 1 else lower
        coded = pl.pallas_call(
            functools.partial(terms_kernel, pairs, (za_size, zb_size)),
            out_shape=pltpu.VMEM((x_size * zb_size, near_rows, LANES), jnp.int16),
            in_specs=[SMEM] + [VMEM] * (SIDES + len(gathered)),
            out_specs=VMEM,
            scratch_shapes=[
                pltpu.VMEM((level, y_size * SIDES + 1, block_rows, LANES), jnp.bfloat16)
            ],
            compiler_params=PARAMS,
            name="local_terms",
        )(table, in_vmem(own), in_vmem(other_lower), *gathered)
        arrived = lax.all_to_all(coded, ("x", "zb"), split_axis=0, concat_axis=0, tiled=True)
        coded = pl.pallas_call(
            functools.partial(middle_kernel, za_size),
            out_shape=pltpu.VMEM((za_size, coded_rows, LANES), jnp.int16),
            in_specs=[VMEM],
            out_specs=VMEM,
            compiler_params=PARAMS,
            name="sum_near",
        )(in_vmem(arrived))
        arrived = lax.all_to_all(coded, "za", split_axis=0, concat_axis=0, tiled=True)
        operands = [mine, swapped] + [in_vmem(array) for array in (dinv, arrived)]
        if level + 1 < levels:
            solution, copies = pl.pallas_call(
                functools.partial(solve_kernel, level),
                out_shape=(pltpu.VMEM((SIDES, block_rows, LANES), jnp.float32), copies_shape),
                in_specs=[VMEM] * 4,
                out_specs=(VMEM, VMEM),
                compiler_params=PARAMS,
                name="solve",
            )(*operands)
            solutions.append(solution)
        else:
            parts = pl.pallas_call(
                last_kernel,
                out_shape=(pltpu.VMEM((levels - 1, block_rows, LANES), jnp.float32),) * SIDES,
                in_specs=[VMEM] * (4 + len(solutions)),
                out_specs=(VMEM,) * SIDES,
                compiler_params=PARAMS,
                name="solve_last",
            )(*operands, *map(in_vmem, solutions))
    halves = lax.all_gather(parts[1], "core", axis=0, tiled=False)
    joined = pl.pallas_call(
        join_kernel,
        out_shape=jax.ShapeDtypeStruct((levels, block_rows, width), jnp.float32),
        in_specs=[VMEM] * 3,
        out_specs=ANY,
        scratch_shapes=[pltpu.SemaphoreType.DMA((1 + SIDES,))],
        compiler_params=PARAMS,
        name="join",
    )(in_vmem(first), in_vmem(parts[0]), in_vmem(halves))
    return joined[:, None, None]


def solution(mesh):
    split = Mesh(mesh.devices.reshape(8, 2, 4, 4, 2), ("y", "core", "x", "za", "zb"))
    row, col = ("y", "core"), ("x", "za", "zb")
    in_specs = (
        P(None, row, col, None, None),
        P(None, row, col, None, None),
        P(None, row, col, None, None, None),
        P(None, row, col, None, None),
    )
    out_specs = P(None, row, col, None, None)
    return jax.shard_map(
        on_device, mesh=split, in_specs=in_specs, out_specs=out_specs, check_vma=False
    )
```

```python
import functools

import jax
import jax.numpy as jnp
from jax import lax
from jax.experimental import pallas as pl
from jax.experimental.pallas import tpu as pltpu
from jax.sharding import Mesh, PartitionSpec as P

LANES = 128
PAD = 8
SIDES = 2
KERNEL_VMEM = 12 << 20
SMALLEST = 2.0**-111
VMEM = pl.BlockSpec(memory_space=pltpu.VMEM)
SMEM = pl.BlockSpec(memory_space=pltpu.SMEM)
ANY = pl.BlockSpec(memory_space=pl.ANY)
PARAMS = pltpu.CompilerParams(vmem_limit_bytes=KERNEL_VMEM)


def in_vmem(array):
    return pltpu.with_memory_space_constraint(array, pltpu.VMEM)


def in_hbm(array):
    return pltpu.with_memory_space_constraint(array, pltpu.HBM)


def code(part):
    largest = jnp.max(jnp.abs(part), axis=0, keepdims=True)
    power = jnp.ceil(jnp.log2(jnp.maximum(largest * 1.001, SMALLEST)))
    coded = jnp.round(part * jnp.exp2(15.0 - power)).astype(jnp.int32)
    return coded.astype(jnp.int16), power


def encode(parts, out_ref, index):
    powers = []
    for side, part in enumerate(parts):
        rows = part.shape[0]
        coded, power = code(part)
        out_ref[index, side * rows : (side + 1) * rows, :] = coded
        powers.append(jnp.broadcast_to(power, (PAD // len(parts), LANES)))
    powers = jnp.concatenate(powers, axis=0).astype(jnp.int32)
    out_ref[index, len(parts) * rows : len(parts) * rows + PAD, :] = powers.astype(jnp.int16)


def decode(block):
    rows = (block.shape[0] - PAD) // SIDES
    powers = block[SIDES * rows :, :].astype(jnp.int32).astype(jnp.float32)
    scales = jnp.exp2(powers - 15.0)
    parts = []
    for side in range(SIDES):
        coded = block[side * rows : (side + 1) * rows, :].astype(jnp.int32).astype(jnp.float32)
        first = side * (PAD // SIDES)
        parts.append(coded * scales[first : first + 1, :])
    return parts


def add_peers(peers, load):
    total = None
    for peer in range(peers):
        parts = decode(load(peer))
        total = parts if total is None else [a + b for a, b in zip(total, parts)]
    return total


def first_kernel(rhs_hbm, dinv_hbm, lower_hbm, sources_ref, *refs):
    solution_ref, mine_ref, sent_ref, factors_ref, rhs_ref, dinv_ref, sems = refs
    copies = [
        pltpu.make_async_copy(rhs_hbm, rhs_ref, sems.at[0]),
        pltpu.make_async_copy(dinv_hbm, dinv_ref, sems.at[1]),
    ]
    early = pltpu.make_async_copy(
        lower_hbm.at[pl.ds(0, factors_ref.shape[0])], factors_ref, sems.at[2]
    )
    for copy in (*copies, early):
        copy.start()
    levels, block_rows, _ = rhs_ref.shape
    base = levels * block_rows
    sent_ref[base:, :] = jnp.zeros((sent_ref.shape[0] - base, LANES), jnp.float32)
    tables = base + (levels - 1) * block_rows
    pairs, per, targets = sources_ref.shape
    for pair in range(pairs):
        rows = slice(tables + pair * per, tables + (pair + 1) * per)
        sent_ref[rows, 0:targets] = sources_ref[pair].astype(jnp.float32)
    for copy in copies:
        copy.wait()
    solution = jnp.dot(
        dinv_ref[0],
        rhs_ref[0].astype(jnp.float32),
        precision=lax.Precision.HIGHEST,
        preferred_element_type=jnp.float32,
    )
    solution_ref[...] = solution
    left_is_mine = lax.axis_index("core") == 0
    for level in range(levels):
        block = rhs_ref[level].astype(jnp.float32) if level else solution
        left, right = block[:, :LANES], block[:, LANES:]
        mine_ref[level] = jnp.where(left_is_mine, left, right).astype(jnp.bfloat16)
        rows = slice(level * block_rows, (level + 1) * block_rows)
        sent_ref[rows, :] = jnp.where(left_is_mine, right, left)
        if level:
            rows = slice(base + (level - 1) * block_rows, base + level * block_rows)
            sent_ref[rows, 0:block_rows] = dinv_ref[level]
    early.wait()


def spread_kernel(mine_ref, swapped_ref, sources_ref, copies_ref, table_ref):
    core = lax.axis_index("core")
    block_rows = mine_ref.shape[1]
    other = swapped_ref.at[1 - core]
    blocks = mine_ref[0], other[0:block_rows, :].astype(jnp.bfloat16)
    for side, block in enumerate(blocks):
        for peer in range(copies_ref.shape[0]):
            copies_ref[peer, side] = block
    none = SIDES * copies_ref.shape[0]

    def places(sources):
        return jnp.where(sources >= 0, jnp.bitwise_xor(sources, core), none)

    pairs, per, targets = sources_ref.shape
    rows = table_ref.shape[1]
    table_ref[0] = jnp.zeros(table_ref.shape[1:], jnp.int32)
    for pair in range(pairs):
        table_ref[0, pair * per : (pair + 1) * per, 0:targets] = places(sources_ref[pair])
    table_ref[1] = places(other[other.shape[0] - rows :, :].astype(jnp.int32))


def terms_kernel(pairs, z_sizes, table_ref, *refs):
    lowers, gathered, (out_ref, blocks_ref) = refs[:SIDES], refs[SIDES:-2], refs[-2:]
    _, targets, block_rows, depth = lowers[0].shape
    per = depth // block_rows
    za_size, zb_size = z_sizes
    none = blocks_ref.shape[1] - 1
    for place, block in enumerate(gathered):
        blocks_ref[place, 0:none] = block[...]
        blocks_ref[place, none] = jnp.zeros(blocks_ref.shape[2:], blocks_ref.dtype)

    def sums(target):
        for side in range(SIDES):
            factors, picked = [], []
            for place, pair in enumerate(pairs):
                factors.append(lowers[side][pair, target])
                for entry in range(per):
                    picked.append(blocks_ref[place, table_ref[side, pair * per + entry, target]])
            yield jnp.dot(
                jnp.concatenate(factors, axis=1),
                jnp.concatenate(picked, axis=0),
                preferred_element_type=jnp.float32,
            )

    tail = za_size * SIDES * block_rows
    for peer in range(targets // za_size):
        x, zb = divmod(peer, zb_size)
        powers, row = [], 0
        for za in range(za_size):
            for part in sums((x * za_size + za) * zb_size + zb):
                coded, power = code(part)
                out_ref[peer, row : row + block_rows, :] = coded
                powers.append(power)
                row += block_rows
        powers = jnp.concatenate(powers, axis=0).astype(jnp.int32)
        out_ref[peer, tail : tail + za_size * SIDES, :] = powers.astype(jnp.int16)


def middle_kernel(za_size, arrived_ref, out_ref):
    peers = arrived_ref.shape[0]
    places = za_size * SIDES
    block_rows = arrived_ref.shape[1] // places - 1
    scales = []
    for peer in range(peers):
        powers = arrived_ref[peer, places * block_rows :, :].astype(jnp.int32)
        scales.append(jnp.exp2(powers.astype(jnp.float32) - 15.0))
    for za in range(za_size):
        parts = []
        for place in range(za * SIDES, (za + 1) * SIDES):
            total = None
            for peer in range(peers):
                block = arrived_ref[peer, place * block_rows : (place + 1) * block_rows, :]
                part = block.astype(jnp.int32).astype(jnp.float32) * scales[peer][place : place + 1, :]
                total = part if total is None else total + part
            parts.append(total)
        encode(parts, out_ref, za)


def solve_parts(level, mine_ref, swapped_ref, dinv_ref, arrived_ref):
    levels, block_rows, _ = mine_ref.shape
    other = swapped_ref.at[1 - lax.axis_index("core")]
    base = (levels + level - 1) * block_rows
    blocks = mine_ref[level].astype(jnp.float32), other[level * block_rows : (level + 1) * block_rows, :]
    factors = dinv_ref[level], other[base : base + block_rows, 0:block_rows]
    total = add_peers(arrived_ref.shape[0], lambda peer: arrived_ref[peer])
    return [
        jnp.dot(
            factor,
            block - part,
            precision=lax.Precision.HIGHEST,
            preferred_element_type=jnp.float32,
        )
        for factor, block, part in zip(factors, blocks, total)
    ]


def solve_kernel(level, mine_ref, swapped_ref, dinv_ref, arrived_ref, solution_ref, copies_ref):
    parts = solve_parts(level, mine_ref, swapped_ref, dinv_ref, arrived_ref)
    for side, part in enumerate(parts):
        solution_ref[side] = part
        for peer in range(copies_ref.shape[0]):
            copies_ref[peer, side] = part.astype(jnp.bfloat16)


def last_kernel(mine_ref, swapped_ref, dinv_ref, arrived_ref, *refs):
    earlier, outs = refs[:-SIDES], refs[-SIDES:]
    for place, ref in enumerate(earlier):
        for side, out_ref in enumerate(outs):
            out_ref[place] = ref[side]
    level = len(earlier) + 1
    parts = solve_parts(level, mine_ref, swapped_ref, dinv_ref, arrived_ref)
    for part, out_ref in zip(parts, outs):
        out_ref[level - 1] = part


def join_kernel(first_ref, mine_ref, swapped_ref, out_ref, sems):
    core = lax.axis_index("core")
    later = pl.ds(1, mine_ref.shape[0])
    copies = [pltpu.make_async_copy(first_ref, out_ref.at[0], sems.at[0])]
    for index, (half, ref) in enumerate(((core, mine_ref), (1 - core, swapped_ref.at[1 - core]))):
        columns = pl.ds(pl.multiple_of(half * LANES, LANES), LANES)
        copies.append(pltpu.make_async_copy(ref, out_ref.at[later, :, columns], sems.at[1 + index]))
    for copy in copies:
        copy.start()
    for copy in copies:
        copy.wait()


def on_device(rhs, dinv, lower, sources):
    levels, _, _, block_rows, width = rhs.shape
    y_size, x_size, za_size, zb_size = (lax.axis_size(name) for name in ("y", "x", "za", "zb"))
    pair_of = {}
    for section in range(levels):
        for target in range(section + 1, levels):
            pair_of[section, target] = len(pair_of)
    rhs, dinv, lower = rhs[:, 0, 0], dinv[:, 0, 0], lower[:, 0, 0]
    sources = jnp.swapaxes(sources[:, 0, 0], 1, 2)
    targets = lower.shape[1]
    coded_rows = SIDES * block_rows + PAD
    near_rows = za_size * SIDES * (block_rows + 1)
    copies_shape = pltpu.VMEM((y_size, SIDES, block_rows, LANES), jnp.bfloat16)

    table_rows = -(-sources.shape[0] * sources.shape[1] // PAD) * PAD
    sent_rows = (2 * levels - 1) * block_rows + table_rows
    first, mine, sent, early = pl.pallas_call(
        first_kernel,
        out_shape=(
            pltpu.VMEM((block_rows, width), jnp.float32),
            pltpu.VMEM((levels, block_rows, LANES), jnp.bfloat16),
            pltpu.VMEM((sent_rows, LANES), jnp.float32),
            pltpu.VMEM((1,) + lower.shape[1:], lower.dtype),
        ),
        in_specs=[ANY, ANY, ANY, VMEM],
        out_specs=(VMEM,) * 4,
        scratch_shapes=[
            pltpu.VMEM(rhs.shape, rhs.dtype),
            pltpu.VMEM(dinv.shape, dinv.dtype),
            pltpu.SemaphoreType.DMA((3,)),
        ],
        compiler_params=PARAMS,
        name="first",
    )(in_hbm(rhs), in_hbm(dinv), in_hbm(lower), in_hbm(sources))
    swapped = in_vmem(lax.all_gather(sent, "core", axis=0, tiled=False))
    mine = in_vmem(mine)
    copies, table = pl.pallas_call(
        spread_kernel,
        out_shape=(copies_shape, pltpu.VMEM((SIDES, table_rows, LANES), jnp.int32)),
        in_specs=[VMEM] * 3,
        out_specs=(VMEM, VMEM),
        compiler_params=PARAMS,
        name="spread",
    )(mine, swapped, sources)
    copies, lower_sent = lax.optimization_barrier((copies, lower))
    other_lower = lax.ppermute(lower_sent, "core", [(0, 1), (1, 0)])

    gathered, solutions = [], []
    for level in range(1, levels):
        blocks = lax.all_to_all(copies, "y", split_axis=0, concat_axis=0, tiled=True)
        gathered.append(in_vmem(blocks.reshape(y_size * SIDES, block_rows, LANES)))
        pairs = tuple(pair_of[earlier, level] for earlier in range(level))
        own = early if level == 1 else lower
        coded = pl.pallas_call(
            functools.partial(terms_kernel, pairs, (za_size, zb_size)),
            out_shape=pltpu.VMEM((x_size * zb_size, near_rows, LANES), jnp.int16),
            in_specs=[SMEM] + [VMEM] * (SIDES + len(gathered)),
            out_specs=VMEM,
            scratch_shapes=[
                pltpu.VMEM((level, y_size * SIDES + 1, block_rows, LANES), jnp.bfloat16)
            ],
            compiler_params=PARAMS,
            name="local_terms",
        )(table, in_vmem(own), in_vmem(other_lower), *gathered)
        arrived = lax.all_to_all(coded, ("x", "zb"), split_axis=0, concat_axis=0, tiled=True)
        coded = pl.pallas_call(
            functools.partial(middle_kernel, za_size),
            out_shape=pltpu.VMEM((za_size, coded_rows, LANES), jnp.int16),
            in_specs=[VMEM],
            out_specs=VMEM,
            compiler_params=PARAMS,
            name="sum_near",
        )(in_vmem(arrived))
        arrived = lax.all_to_all(coded, "za", split_axis=0, concat_axis=0, tiled=True)
        operands = [mine, swapped] + [in_vmem(array) for array in (dinv, arrived)]
        if level + 1 < levels:
            solution, copies = pl.pallas_call(
                functools.partial(solve_kernel, level),
                out_shape=(pltpu.VMEM((SIDES, block_rows, LANES), jnp.float32), copies_shape),
                in_specs=[VMEM] * 4,
                out_specs=(VMEM, VMEM),
                compiler_params=PARAMS,
                name="solve",
            )(*operands)
            solutions.append(solution)
        else:
            parts = pl.pallas_call(
                last_kernel,
                out_shape=(pltpu.VMEM((levels - 1, block_rows, LANES), jnp.float32),) * SIDES,
                in_specs=[VMEM] * (4 + len(solutions)),
                out_specs=(VMEM,) * SIDES,
                compiler_params=PARAMS,
                name="solve_last",
            )(*operands, *map(in_vmem, solutions))
    halves = lax.all_gather(parts[1], "core", axis=0, tiled=False)
    joined = pl.pallas_call(
        join_kernel,
        out_shape=jax.ShapeDtypeStruct((levels, block_rows, width), jnp.float32),
        in_specs=[VMEM] * 3,
        out_specs=ANY,
        scratch_shapes=[pltpu.SemaphoreType.DMA((1 + SIDES,))],
        compiler_params=PARAMS,
        name="join",
    )(in_vmem(first), in_vmem(parts[0]), in_vmem(halves))
    return joined[:, None, None]


def solution(mesh):
    split = Mesh(mesh.devices.reshape(8, 2, 4, 4, 2), ("y", "core", "x", "za", "zb"))
    row, col = ("y", "core"), ("x", "za", "zb")
    in_specs = (
        P(None, row, col, None, None),
        P(None, row, col, None, None),
        P(None, row, col, None, None, None),
        P(None, row, col, None, None),
    )
    out_specs = P(None, row, col, None, None)
    return jax.shard_map(
        on_device, mesh=split, in_specs=in_specs, out_specs=out_specs, check_vma=False
    )
```
